32 devices in a mesh: dp: 4 (over y, core), tensor: 8 (over z, x).
Axes of the slice: x: 2, y: 2, z: 4, core: 2. Of those that a mesh axis runs over, the one named last changes fastest.
Arguments:
- src_ids: int32 [1024, 4], P('tensor', 'dp'), may hold values from 0 to 131071, as said below
- tgt_ids: int32 [1024, 4], P('tensor', 'dp'), may hold values from 0 to 131071, as said below
- src_segs: int32 [1024, 4], P(None, 'dp'), may hold values from -1 to 4, as said below
- tgt_segs: int32 [1024, 4], P(None, 'dp'), may hold values from -1 to 4, as said below
- embed_table: bfloat16 [131072, 1024], P(('dp', 'tensor')), may hold values from -6 to 6
- norm_gains: float32 [9, 1024], replicated, may hold values from 0.5 to 1.5
- enc_qkv: bfloat16 [3, 1024, 1024], P(None, None, 'tensor'), may hold values from -0.1875 to 0.1875
- enc_out: bfloat16 [1024, 1024], P('tensor'), may hold values from -1.5 to 1.5
- enc_up: bfloat16 [1024, 4096], P(None, 'tensor'), may hold values from -0.1875 to 0.1875
- enc_down: bfloat16 [4096, 1024], P('tensor'), may hold values from -0.09375 to 0.09375
- dec_qkv: bfloat16 [3, 1024, 1024], P(None, None, 'tensor'), may hold values from -0.1875 to 0.1875
- dec_out: bfloat16 [1024, 1024], P('tensor'), may hold values from -1.5 to 1.5
- cross_q: bfloat16 [1024, 1024], P(None, 'tensor'), may hold values from -0.1875 to 0.1875
- cross_kv: bfloat16 [2, 1024, 1024], P(None, None, 'tensor'), may hold values from -0.1875 to 0.1875
- cross_out: bfloat16 [1024, 1024], P('tensor'), may hold values from -1.5 to 1.5
- dec_up: bfloat16 [1024, 4096], P(None, 'tensor'), may hold values from -0.1875 to 0.1875
- dec_down: bfloat16 [4096, 1024], P('tensor'), may hold values from -0.09375 to 0.09375
- cotangent: float32 [1024, 4, 1024], P('tensor', 'dp'), may hold values from -6 to 6
Outputs:
- decoded: float32 [1024, 4, 1024], P('tensor', 'dp')
- table_grad: float32 [131072, 1024], P(('dp', 'tensor'))
- gain_grad: float32 [9, 1024], replicated
- enc_qkv_grad: float32 [3, 1024, 1024], P(None, 'dp', 'tensor')
- enc_out_grad: float32 [1024, 1024], P('tensor', 'dp')
- enc_up_grad: float32 [1024, 4096], P('dp', 'tensor')
- enc_down_grad: float32 [4096, 1024], P('tensor', 'dp')
- dec_qkv_grad: float32 [3, 1024, 1024], P(None, 'dp', 'tensor')
- dec_out_grad: float32 [1024, 1024], P('tensor', 'dp')
- cross_q_grad: float32 [1024, 1024], P('dp', 'tensor')
- cross_kv_grad: float32 [2, 1024, 1024], P(None, 'dp', 'tensor')
- cross_out_grad: float32 [1024, 1024], P('tensor', 'dp')
- dec_up_grad: float32 [1024, 4096], P('dp', 'tensor')
- dec_down_grad: float32 [4096, 1024], P('tensor', 'dp')
The draws below stay inside these ranges and needn't reach their ends.
Inputs may be any that keep to these rules, and one draw needn't show every extreme that they name: `src_ids`: of the 256 source and target tokens that one device holds, at most 12 have ids in one block of 4096 consecutive table rows, and in every device's tokens one such block holds exactly 12. `tgt_ids`: drawn together with src_ids under the bound stated there. `src_segs`: each row holds 5 documents numbered 0 to 4 in order, each of 128 to 191 positions, then padding marked -1 on one position or more. `tgt_segs`: laid out as the source segments; document k of a target row translates document k of the same source row.
All inputs are finite; a program needn't handle non-finite values.
Results may differ from the reference program's by a relative error of at most 0.035.
Values may be sent and summed in bfloat16 or wider, within the bound.
No kernel may reach another device: no remote copies, remote signals or barrier semaphores. Data moves between devices by JAX's collectives and lax.ppermute only.
A program may use at most 192 MiB of HBM per device.

```python
import math
from functools import partial
import jax
import jax.numpy as jnp
from jax import lax

D = 1024
HEADS = 16
FF = 4096
HEAD_DIM = 64
VOCAB = 131072
NORMS = 9
SEQ = 1024
DOCS = 5
ROWS_DEV = 1
ROWS = 4
TOK_BLOCK = 256
SHARD_ROWS = 4096
CAP = 12


def owner_blocks(base_key):
    owner_count = VOCAB // SHARD_ROWS
    seq_local = TOK_BLOCK // (2 * ROWS_DEV)
    group_dp = ROWS // ROWS_DEV
    group_tensor = SEQ // seq_local

    def one_block(block_key):
        key_full, key_rest, key_shuffle, key_within = jax.random.split(block_key, 4)
        full_owner = jax.random.randint(key_full, (), 0, owner_count).astype(jnp.int32)
        others = jax.random.permutation(key_rest, (owner_count - 1) * CAP)[:TOK_BLOCK - CAP].astype(jnp.int32) // CAP
        others = others + (others >= full_owner).astype(jnp.int32)
        owners = jnp.concatenate([jnp.full((CAP,), full_owner, jnp.int32), others])
        owners = owners[jax.random.permutation(key_shuffle, TOK_BLOCK)]
        within = jax.random.randint(key_within, (TOK_BLOCK,), 0, SHARD_ROWS).astype(jnp.int32)
        return (owners * SHARD_ROWS + within).astype(jnp.int32)
    block_keys = jax.random.split(jax.random.fold_in(base_key, 11), group_dp * group_tensor)
    blocks = jax.vmap(one_block)(block_keys)
    return blocks.reshape(group_dp, group_tensor, 2, seq_local, ROWS_DEV)


def arrange(blocks, stream):
    chosen = blocks[:, :, stream]
    return chosen.transpose(1, 2, 0, 3).reshape(SEQ, ROWS).astype(jnp.int32)


def draw_src_ids(key, part):
    return arrange(owner_blocks(key), 0)


def draw_tgt_ids(key, part):
    return arrange(owner_blocks(key), 1)


def doc_segments(base_key):
    lengths = SEQ // 8 + jax.random.randint(base_key, (ROWS, DOCS), 0, SEQ // 16)
    doc_ends = jnp.cumsum(lengths, axis=1)
    positions = jnp.arange(SEQ)
    passed = jnp.sum((positions[None, :, None] >= doc_ends[:, None, :]).astype(jnp.int32), axis=2)
    labels = jnp.where(passed >= DOCS, -1, passed)
    return labels.T.astype(jnp.int32)


def draw_src_segs(key, part):
    return doc_segments(jax.random.fold_in(key, 3))


def draw_tgt_segs(key, part):
    return doc_segments(jax.random.fold_in(key, 5))


def level_of(key, shape, pieces, least, largest):
    loudness, own = 1.0, jax.random.fold_in(key, 6)
    for position, blocks in pieces:
        draws = jnp.exp(jax.random.uniform(jax.random.fold_in(own, position), (blocks,), jnp.float32, least / len(pieces), largest / len(pieces)))
        loudness = loudness * jnp.repeat(draws, shape[position] // blocks).reshape([-1 if axis == position else 1 for axis in range(len(shape))])
    return loudness


def noise(stream_key, extent, width, reach, shards=(), dtype=jnp.bfloat16):
    values = jax.random.normal(stream_key, extent, jnp.float32) * width
    if len(shards) > 0:
        values = level_of(stream_key, extent, shards, -0.22, 0.18) * values
    return jnp.clip(values, min=-reach, max=reach).astype(dtype)


def setup_inputs(seed: int = 0) -> dict:
    key_of = jax.random.split(jax.random.key(seed), 19)
    src_ids = draw_src_ids(jax.random.fold_in(key_of[18], 71), 0)
    tgt_ids = draw_tgt_ids(jax.random.fold_in(key_of[18], 71), 0)
    src_segs = draw_src_segs(jax.random.fold_in(key_of[18], 71), 0)
    tgt_segs = draw_tgt_segs(jax.random.fold_in(key_of[18], 71), 0)
    embed_table = noise(key_of[4], (VOCAB, D), 1.0, 6.0, ((0, 32),))
    norm_gains = jnp.clip(1.0 + 0.1 * jax.random.normal(key_of[5], (NORMS, D), jnp.float32), 0.5, 1.5)
    enc_qkv = noise(key_of[6], (3, D, D), D ** -0.5, 0.1875, ((2, 8),))
    enc_out = noise(key_of[7], (D, D), (max(1, D // 64)) ** -0.5, 1.5, ((0, 8),))
    enc_up = noise(key_of[8], (D, FF), D ** -0.5, 0.1875, ((1, 8),))
    enc_down = noise(key_of[9], (FF, D), FF ** -0.5, 0.09375, ((0, 8),))
    dec_qkv = noise(key_of[10], (3, D, D), D ** -0.5, 0.1875, ((2, 8),))
    dec_out = noise(key_of[11], (D, D), (max(1, D // 64)) ** -0.5, 1.5, ((0, 8),))
    cross_q = noise(key_of[12], (D, D), D ** -0.5, 0.1875, ((1, 8),))
    cross_kv = noise(key_of[13], (2, D, D), D ** -0.5, 0.1875, ((2, 8),))
    cross_out = noise(key_of[14], (D, D), (max(1, D // 64)) ** -0.5, 1.5, ((0, 8),))
    dec_up = noise(key_of[15], (D, FF), D ** -0.5, 0.1875, ((1, 8),))
    dec_down = noise(key_of[16], (FF, D), FF ** -0.5, 0.09375, ((0, 8),))
    cotangent = noise(key_of[17], (SEQ, ROWS, D), 1.0, 6.0, ((0, 8), (1, 4)), jnp.float32)
    return dict(src_ids=src_ids, tgt_ids=tgt_ids, src_segs=src_segs, tgt_segs=tgt_segs, embed_table=embed_table, norm_gains=norm_gains, enc_qkv=enc_qkv, enc_out=enc_out, enc_up=enc_up, enc_down=enc_down, dec_qkv=dec_qkv, dec_out=dec_out, cross_q=cross_q, cross_kv=cross_kv, cross_out=cross_out, dec_up=dec_up, dec_down=dec_down, cotangent=cotangent)


@jax.custom_vjp
def low(v):
    return lax.optimization_barrier(v.astype(jnp.bfloat16)).astype(jnp.float32)

@jax.custom_vjp
def low_back(v):
    return v

def low_keep(v):
    return (low(v), None)

def low_pass(kept, grad):
    return (grad,)

def back_keep(v):
    return (v, None)

def back_low(kept, grad):
    return (low(grad),)
low.defvjp(low_keep, low_pass)
low_back.defvjp(back_keep, back_low)
NORM_EPS = 1e-05
MASKED = -1e+30
HIGHEST = lax.Precision.HIGHEST

def layer_norm(values, gain_row):
    centre = lax.optimization_barrier(jnp.mean(values, axis=-1, keepdims=True))
    shifted = values - centre
    spread = lax.optimization_barrier(jnp.mean(shifted * shifted, axis=-1, keepdims=True))
    return shifted * lax.rsqrt(spread + NORM_EPS) * gain_row

def rounded(values):
    return low(low_back(values))

def project(values, weight):
    return jnp.einsum('srd,de->sre', values, weight, precision=HIGHEST)

def attend_row(queries, keys_in, values_in, seg_query, seg_key, causal):
    factor = 1.0 / math.sqrt(HEAD_DIM)
    scores = low_back(jnp.einsum('qhd,khd->hqk', queries, keys_in, precision=HIGHEST) * factor)
    allowed = (seg_query[:, None] == seg_key[None, :]) | (seg_query[:, None] < 0)
    if causal:
        allowed = allowed & (jnp.arange(SEQ)[:, None] >= jnp.arange(SEQ)[None, :])
    scores = jnp.where(allowed[None], scores, MASKED)
    attn_probs = low(jax.nn.softmax(scores, axis=-1))
    return jnp.einsum('hqk,khd->qhd', attn_probs, values_in, precision=HIGHEST)

def heads_first(arranged):
    return arranged.reshape(arranged.shape[0], arranged.shape[1], HEADS, HEAD_DIM).transpose(1, 0, 2, 3)

def attention(queries, keys_in, values_in, seg_query, seg_key, causal):
    per_row = jax.checkpoint(partial(attend_row, causal=causal))

    def one_row(packed):
        return per_row(packed[0], packed[1], packed[2], packed[3], packed[4])
    mixed_rows = lax.map(one_row, (heads_first(queries), heads_first(keys_in), heads_first(values_in), seg_query.T, seg_key.T))
    return mixed_rows.transpose(1, 0, 2, 3).reshape(queries.shape)

def self_block(normed, qkv_weight, out_weight, segments, causal):
    queries = rounded(project(normed, qkv_weight[0]))
    keys_in = rounded(project(normed, qkv_weight[1]))
    values_in = rounded(project(normed, qkv_weight[2]))
    mixed_heads = rounded(attention(queries, keys_in, values_in, segments, segments, causal))
    return low_back(project(mixed_heads, out_weight))

def cross_block(normed, memory, query_weight, pair_weight, out_weight, seg_target, seg_source):
    queries = rounded(project(normed, query_weight))
    keys_in = rounded(project(memory, pair_weight[0]))
    values_in = rounded(project(memory, pair_weight[1]))
    mixed_heads = rounded(attention(queries, keys_in, values_in, seg_target, seg_source, False))
    return low_back(project(mixed_heads, out_weight))

def feed_forward(normed, up_weight, down_weight):
    pre_act = low_back(project(normed, up_weight))
    activated = low(jax.nn.gelu(pre_act, approximate=False))
    return low_back(project(activated, down_weight))

def embed(table_wide, token_ids, live_mask, gain_row):
    token_rows = jnp.take(table_wide, token_ids, axis=0) * live_mask[..., None]
    return layer_norm(token_rows * math.sqrt(D), gain_row)

def forward_layer(params, table_wide, src_ids, tgt_ids, src_segs, tgt_segs):
    norm_gains, enc_qkv, enc_out, enc_up, enc_down, dec_qkv, dec_out, cross_q, cross_kv, cross_out, dec_up, dec_down = params
    src_live = (src_segs >= 0).astype(jnp.float32)
    tgt_live = (tgt_segs >= 0).astype(jnp.float32)
    hidden = embed(table_wide, src_ids, src_live, norm_gains[0])
    hidden = hidden + self_block(low(layer_norm(hidden, norm_gains[1])), enc_qkv, enc_out, src_segs, False)
    hidden = hidden + feed_forward(low(layer_norm(hidden, norm_gains[2])), enc_up, enc_down)
    memory = low(layer_norm(hidden, norm_gains[3]))
    dec_state = embed(table_wide, tgt_ids, tgt_live, norm_gains[4])
    dec_state = dec_state + self_block(low(layer_norm(dec_state, norm_gains[5])), dec_qkv, dec_out, tgt_segs, True)
    dec_state = dec_state + cross_block(low(layer_norm(dec_state, norm_gains[6])), memory, cross_q, cross_kv, cross_out, tgt_segs, src_segs)
    dec_state = dec_state + feed_forward(low(layer_norm(dec_state, norm_gains[7])), dec_up, dec_down)
    return layer_norm(dec_state, norm_gains[8]) * tgt_live[..., None]

def reference(src_ids, tgt_ids, src_segs, tgt_segs, embed_table, norm_gains, enc_qkv, enc_out, enc_up, enc_down, dec_qkv, dec_out, cross_q, cross_kv, cross_out, dec_up, dec_down, cotangent):
    params = (norm_gains.astype(jnp.float32), enc_qkv.astype(jnp.float32), enc_out.astype(jnp.float32), enc_up.astype(jnp.float32), enc_down.astype(jnp.float32), dec_qkv.astype(jnp.float32), dec_out.astype(jnp.float32), cross_q.astype(jnp.float32), cross_kv.astype(jnp.float32), cross_out.astype(jnp.float32), dec_up.astype(jnp.float32), dec_down.astype(jnp.float32))
    table_wide = embed_table.astype(jnp.float32)

    def run_layer(param_set, table_set):
        return forward_layer(param_set, table_set, src_ids, tgt_ids, src_segs, tgt_segs)
    decoded, pull_back = jax.vjp(run_layer, params, table_wide)
    param_grads, table_sums = pull_back(cotangent.astype(jnp.float32))
    src_live = (src_segs >= 0).astype(jnp.float32)
    tgt_live = (tgt_segs >= 0).astype(jnp.float32)
    counts = jnp.zeros((VOCAB,), jnp.float32).at[src_ids.reshape(-1)].add(src_live.reshape(-1))
    counts = counts.at[tgt_ids.reshape(-1)].add(tgt_live.reshape(-1))
    table_grad = table_sums / jnp.maximum(counts, 1.0)[:, None]
    return (decoded, table_grad, param_grads[0], param_grads[1], param_grads[2], param_grads[3], param_grads[4], param_grads[5], param_grads[6], param_grads[7], param_grads[8], param_grads[9], param_grads[10], param_grads[11])
```

```python
import math
from functools import partial

import jax
import jax.numpy as jnp
from jax import lax
from jax.experimental import pallas as pl
from jax.experimental.pallas import tpu as pltpu
from jax.sharding import PartitionSpec as P

HEAD_DIM = 64
FACTOR = 0.125

NORM_EPS = 1e-05
MASKED = -1e30
F32 = jnp.float32
BF16 = jnp.bfloat16
VMEM_LIMIT = 48 << 20


def layer_norm(values, gain_row):
    centre = jnp.mean(values, axis=-1, keepdims=True)
    shifted = values - centre
    spread = jnp.mean(shifted * shifted, axis=-1, keepdims=True)
    return shifted * lax.rsqrt(spread + NORM_EPS) * gain_row


def embed_norm(token_rows, gain_row):
    return layer_norm(token_rows * math.sqrt(token_rows.shape[-1]), gain_row)


def gelu_pair(pre_act):
    phi_big = 0.5 * (1.0 + lax.erf(pre_act * (1.0 / math.sqrt(2.0))))
    phi_small = jnp.exp(-0.5 * pre_act * pre_act) * (1.0 / math.sqrt(2.0 * math.pi))
    return pre_act * phi_big, phi_big + pre_act * phi_small


def dot(lhs, rhs, dims):
    return lax.dot_general(lhs, rhs, (dims, ((), ())), preferred_element_type=F32)


NN = ((1,), (0,))
NT = ((1,), (1,))
TN = ((0,), (0,))


def allowed_block(seg_query, seg_key, pos_query, pos_key, causal):
    allowed = (seg_key == seg_query) | (seg_query < 0)
    if causal:
        allowed = allowed & (pos_query >= pos_key)
    return allowed


def attn_fwd_kernel(q_ref, k_ref, v_ref, sq_ref, sk_ref, pq_ref, pk_ref, o_ref, st_ref, *, causal, heads):
    allowed = allowed_block(sq_ref[...], sk_ref[...], pq_ref[...], pk_ref[...], causal)
    for head in range(heads):
        cols = slice(head * HEAD_DIM, (head + 1) * HEAD_DIM)
        scores = dot(k_ref[:, cols], q_ref[:, cols], NT)
        scores = jnp.where(allowed, scores, MASKED)
        peak = jnp.max(scores, axis=0, keepdims=True)
        raised = jnp.exp(scores - peak)
        inverse = 1.0 / jnp.sum(raised, axis=0, keepdims=True)
        probs = (raised * inverse).astype(BF16)
        mixed = dot(v_ref[:, cols], probs, TN)
        o_ref[:, cols] = mixed.T.astype(BF16)
        st_ref[head : head + 1, :] = peak
        st_ref[heads + head : heads + head + 1, :] = inverse


def attn_bwd_kernel(
    q_ref, k_ref, v_ref, g_ref, sq_ref, sk_ref, pq_ref, pk_ref, st_ref, dq_ref, dk_ref, dv_ref, *, causal, heads
):
    @pl.when(pl.program_id(0) == 0)
    def _():
        dk_ref[...] = jnp.zeros_like(dk_ref)
        dv_ref[...] = jnp.zeros_like(dv_ref)

    allowed = allowed_block(sq_ref[...], sk_ref[...], pq_ref[...], pk_ref[...], causal)
    for head in range(heads):
        cols = slice(head * HEAD_DIM, (head + 1) * HEAD_DIM)
        queries, keys, values, grads = q_ref[:, cols], k_ref[:, cols], v_ref[:, cols], g_ref[:, cols]
        scores = jnp.where(allowed, dot(keys, queries, NT), MASKED)
        probs = jnp.exp(scores - st_ref[head : head + 1, :]) * st_ref[heads + head : heads + head + 1, :]
        grad_probs = dot(values, grads, NT)
        inner = jnp.sum(probs * grad_probs, axis=0, keepdims=True)
        grad_scores = (probs * (grad_probs - inner)).astype(BF16)
        dq_ref[:, cols] = (dot(keys, grad_scores, TN) * FACTOR).T.astype(BF16)
        dk_ref[:, cols] += dot(grad_scores, queries, NN)
        dv_ref[:, cols] += dot(probs.astype(BF16), grads, NN)


def mask_specs(step, keys_len):
    return [
        pl.BlockSpec((1, step), lambda i: (0, i)),
        pl.BlockSpec((keys_len, 1), lambda i: (0, 0)),
        pl.BlockSpec((1, step), lambda i: (0, i)),
        pl.BlockSpec((keys_len, 1), lambda i: (0, 0)),
    ]


def attend(queries, keys, values, marks, causal):
    length, width = queries.shape
    keys_len = keys.shape[0]
    heads = width // HEAD_DIM
    step = min(256, length)
    rows = pl.BlockSpec((step, width), lambda i: (i, 0))
    whole = pl.BlockSpec((keys_len, width), lambda i: (0, 0))
    return pl.pallas_call(
        partial(attn_fwd_kernel, causal=causal, heads=heads),
        grid=(length // step,),
        in_specs=[rows, whole, whole] + mask_specs(step, keys_len),
        out_specs=[rows, pl.BlockSpec((2 * heads, step), lambda i: (0, i))],
        out_shape=[
            jax.ShapeDtypeStruct((length, width), BF16),
            jax.ShapeDtypeStruct((2 * heads, length), F32),
        ],
        compiler_params=pltpu.CompilerParams(vmem_limit_bytes=VMEM_LIMIT),
        cost_estimate=pl.CostEstimate(
            flops=4 * length * keys_len * width, transcendentals=length * keys_len * heads,
            bytes_accessed=4 * (length + keys_len) * width
        ),
        name="attend",
    )(queries, keys, values, *marks)


def attend_back(queries, keys, values, grad_mixed, marks, stats, causal):
    length, width = queries.shape
    keys_len = keys.shape[0]
    heads = width // HEAD_DIM
    step = min(256, length)
    rows = pl.BlockSpec((step, width), lambda i: (i, 0))
    whole = pl.BlockSpec((keys_len, width), lambda i: (0, 0))
    return pl.pallas_call(
        partial(attn_bwd_kernel, causal=causal, heads=heads),
        grid=(length // step,),
        in_specs=[rows, whole, whole, rows]
        + mask_specs(step, keys_len)
        + [pl.BlockSpec((2 * heads, step), lambda i: (0, i))],
        out_specs=[rows, whole, whole],
        out_shape=[
            jax.ShapeDtypeStruct((length, width), BF16),
            jax.ShapeDtypeStruct((keys_len, width), F32),
            jax.ShapeDtypeStruct((keys_len, width), F32),
        ],
        compiler_params=pltpu.CompilerParams(vmem_limit_bytes=VMEM_LIMIT),
        cost_estimate=pl.CostEstimate(
            flops=10 * length * keys_len * width, transcendentals=length * keys_len * heads,
            bytes_accessed=10 * (length + keys_len) * width
        ),
        name="attend_back",
    )(queries, keys, values, grad_mixed, *marks, stats)


class Places:
    def __init__(self):
        self.dp_size = lax.axis_size("dp")
        self.tensor_size = lax.axis_size("tensor")
        self.group = self.tensor_size // 2
        self.dp_index = lax.axis_index("dp")
        tensor_index = lax.axis_index("tensor")
        self.core = self.dp_index % 2
        self.place = tensor_index % self.group

    def swap(self, value):
        pairs = []
        for dp_index in range(self.dp_size):
            for tensor_index in range(self.tensor_size):
                pair, core = divmod(dp_index, 2)
                side, place = divmod(tensor_index, self.group)
                pairs.append(
                    (
                        dp_index * self.tensor_size + tensor_index,
                        (2 * pair + side) * self.tensor_size + core * self.group + place,
                    )
                )
        return lax.ppermute(value, ("dp", "tensor"), pairs)

    def other_core(self, value):
        return lax.ppermute(value, "dp", [(d, d ^ 1) for d in range(self.dp_size)])

    def partner(self, value):
        return lax.ppermute(value, "tensor", [(t, t ^ self.group) for t in range(self.tensor_size)])

    def mate(self, value, offset):
        return lax.ppermute(value, "tensor", [(t, t ^ offset) for t in range(self.tensor_size)])

    def gather(self, block):
        if self.group == 4:
            half = block.shape[0] // 2
            low, high = block[:half], block[half:]
            low_1, high_2 = self.mate(low, 1), self.mate(high, 2)
            high_1, low_2 = self.mate(high, 1), self.mate(low, 2)
            high_3, low_3 = self.mate(high_2, 1), self.mate(low_1, 2)
            return jnp.concatenate([block, low_1, high_1, low_2, high_2, low_3, high_3])
        return jnp.concatenate([block] + [self.mate(block, o) for o in range(1, self.group)])

    def scatter_sum(self, value):
        length = value.shape[0] // self.group
        total = value[:length]
        for offset in range(1, self.group):
            sent = value[offset * length : (offset + 1) * length].astype(BF16)
            total = total + self.mate(sent, offset).astype(F32)
        return total

    def partner_weight(self, stacked):
        rows = stacked.shape[0] // self.dp_size
        share = lax.dynamic_slice_in_dim(stacked, self.dp_index * rows, rows, 0)
        return lax.all_gather(self.partner(share), "dp", axis=0, tiled=True)

    def sum_weight(self, own, other, axis):
        summed = lax.psum_scatter(
            jnp.stack([own.astype(BF16), other.astype(BF16)]), "dp", scatter_dimension=axis + 1, tiled=True
        )
        return summed[0].astype(F32) + self.partner(summed[1]).astype(F32)

    def marks(self, seg_row, seg_key_row):
        length = seg_row.shape[0] // self.tensor_size
        order = self.place ^ jnp.arange(self.group)
        own = self.core * self.group + order
        keys = jnp.concatenate([own, (1 - self.core) * self.group + order])

        def positions(blocks):
            return (blocks[:, None] * length + jnp.arange(length)[None, :]).reshape(-1)

        def segments(row, blocks):
            return jnp.take(row.reshape(-1, length), blocks, axis=0).reshape(-1)

        return (
            segments(seg_row, own)[None, :],
            segments(seg_key_row, keys)[:, None],
            positions(own)[None, :],
            positions(keys)[:, None],
        )


def project(gathered, weights):
    return [dot(gathered, weight, NN).astype(BF16) for weight in weights]


def add_up(terms):
    total = terms[0]
    for term in terms[1:]:
        total = total + term
    return total


def both_cores(places, first, second):
    width = first.shape[1]
    other = places.other_core(jnp.concatenate([first, second], axis=1))
    return jnp.concatenate([first, other[:, :width]]), jnp.concatenate([second, other[:, width:]])


def both_cores_sum(places, first, second):
    width, half = first.shape[1], first.shape[0] // 2
    sent = jnp.concatenate([first[half:].astype(BF16), second[half:].astype(BF16)], axis=1)
    other = places.other_core(sent).astype(F32)
    return (first[:half] + other[:, :width]).astype(BF16), (second[:half] + other[:, width:]).astype(BF16)


def attention_forward(places, hidden, gain_row, qkv, out_weight, marks, causal):
    normed, norm_back = jax.vjp(layer_norm, hidden, gain_row)
    gathered = places.gather(normed.astype(BF16))
    queries, keys, values = project(gathered, qkv)
    queries = queries * jnp.asarray(FACTOR, BF16)
    keys, values = both_cores(places, keys, values)
    mixed, stats = attend(queries, keys, values, marks, causal)
    update = places.scatter_sum(dot(mixed, out_weight, NN))
    return hidden + update, (norm_back, gathered, queries, keys, values, mixed, stats)


def attention_backward(places, grad_hidden, saved, qkv, out_weight, marks, causal):
    norm_back, gathered, queries, keys, values, mixed, stats = saved
    grad_full = places.gather(grad_hidden.astype(BF16))
    grad_mixed = dot(grad_full, out_weight, NT).astype(BF16)
    grad_q, grad_k, grad_v = attend_back(queries, keys, values, grad_mixed, marks, stats, causal)
    grad_k, grad_v = both_cores_sum(places, grad_k, grad_v)
    grads = [grad_q, grad_k, grad_v]
    grad_normed = places.scatter_sum(add_up([dot(g, w, NT) for g, w in zip(grads, qkv)]))
    grad_input, gain_grad = norm_back(grad_normed)
    out_grad = dot(mixed, grad_full, TN)
    qkv_grad = [dot(gathered, g, TN) for g in grads]
    return grad_hidden + grad_input, gain_grad, qkv_grad, out_grad


def cross_forward(places, state, gain_row, memory_full, query_weight, pair, out_weight, marks):
    normed, norm_back = jax.vjp(layer_norm, state, gain_row)
    gathered = places.gather(normed.astype(BF16))
    queries = project(gathered, [query_weight])[0] * jnp.asarray(FACTOR, BF16)
    keys, values = both_cores(places, *project(memory_full, pair))
    mixed, stats = attend(queries, keys, values, marks, False)
    update = places.scatter_sum(dot(mixed, out_weight, NN))
    return state + update, (norm_back, gathered, queries, keys, values, mixed, stats)


def cross_backward(places, grad_state, saved, memory_full, query_weight, pair, out_weight, marks):
    norm_back, gathered, queries, keys, values, mixed, stats = saved
    grad_full = places.gather(grad_state.astype(BF16))
    grad_mixed = dot(grad_full, out_weight, NT).astype(BF16)
    grad_q, grad_k, grad_v = attend_back(queries, keys, values, grad_mixed, marks, stats, False)
    grad_k, grad_v = both_cores_sum(places, grad_k, grad_v)
    grad_memory = places.scatter_sum(dot(grad_k, pair[0], NT) + dot(grad_v, pair[1], NT))
    grad_normed = places.scatter_sum(dot(grad_q, query_weight, NT))
    grad_input, gain_grad = norm_back(grad_normed)
    out_grad = dot(mixed, grad_full, TN)
    query_grad = dot(gathered, grad_q, TN)
    pair_grad = [dot(memory_full, g, TN) for g in (grad_k, grad_v)]
    return grad_state + grad_input, gain_grad, grad_memory, query_grad, pair_grad, out_grad


def ffn_forward(places, hidden, gain_row, ups, downs):
    normed, norm_back = jax.vjp(layer_norm, hidden, gain_row)
    gathered = places.gather(normed.astype(BF16))
    acts, slopes = [], []
    for up in ups:
        act, slope = gelu_pair(dot(gathered, up, NN))
        acts.append(act.astype(BF16))
        slopes.append(slope)
    update = places.scatter_sum(add_up([dot(a, w, NN) for a, w in zip(acts, downs)]))
    return hidden + update, (norm_back, gathered, acts, slopes)


def ffn_backward(places, grad_hidden, saved, ups, downs):
    norm_back, gathered, acts, slopes = saved
    grad_full = places.gather(grad_hidden.astype(BF16))
    grad_pre = [(s * dot(grad_full, w, NT)).astype(BF16) for s, w in zip(slopes, downs)]
    grad_normed = places.scatter_sum(add_up([dot(g, w, NT) for g, w in zip(grad_pre, ups)]))
    grad_input, gain_grad = norm_back(grad_normed)
    down_grads = [dot(a, grad_full, TN) for a in acts]
    up_grads = [dot(gathered, g, TN) for g in grad_pre]
    return grad_hidden + grad_input, gain_grad, up_grads, down_grads


def table_lookup(src_ids, tgt_ids, src_live, tgt_live, embed_table):
    token_ids = jnp.concatenate([src_ids.reshape(-1), tgt_ids.reshape(-1)])
    token_live = jnp.concatenate([src_live.reshape(-1), tgt_live.reshape(-1)])
    shard_rows = embed_table.shape[0]
    size_dp = lax.axis_size("dp")
    size_tensor = lax.axis_size("tensor")
    owners = size_dp * size_tensor
    capacity = max(2, 3 * token_ids.shape[0] // (2 * owners))
    owner_of = token_ids // shard_rows
    row_of = token_ids - owner_of * shard_rows
    owner_flags = ((owner_of[:, None] == jnp.arange(owners)[None, :]) & token_live[:, None]).astype(
        jnp.int32
    )
    earlier = jnp.cumsum(owner_flags, axis=0) - owner_flags
    ranking = jnp.sum(earlier * owner_flags, axis=1)
    slot_of = jnp.where(token_live, owner_of * capacity + ranking, owners * capacity)
    requests = jnp.full((owners * capacity,), -1, jnp.int32).at[slot_of].set(row_of, mode="drop")
    wanted = lax.all_to_all(
        lax.all_to_all(
            requests.reshape(size_dp, size_tensor, capacity),
            "dp",
            split_axis=0,
            concat_axis=0,
            tiled=True,
        ),
        "tensor",
        split_axis=1,
        concat_axis=1,
        tiled=True,
    ).reshape(-1)
    found_rows = wanted >= 0
    picked = jnp.take(embed_table, jnp.where(found_rows, wanted, 0), axis=0)
    picked = jnp.where(found_rows[:, None], picked, jnp.zeros_like(picked))
    replies = lax.all_to_all(
        lax.all_to_all(
            picked.reshape(size_dp, size_tensor, capacity, -1),
            "dp",
            split_axis=0,
            concat_axis=0,
            tiled=True,
        ),
        "tensor",
        split_axis=1,
        concat_axis=1,
        tiled=True,
    )
    replies = replies.reshape(owners * capacity, -1)
    fetched = jnp.take(replies, jnp.minimum(slot_of, owners * capacity - 1), axis=0).astype(
        jnp.float32
    )
    fetched = fetched * token_live[:, None].astype(jnp.float32)
    return (fetched, (slot_of, wanted, found_rows, size_dp, size_tensor, capacity))


def table_gradient(grad_tokens, route_info, shard_rows):
    slot_of, wanted, found_rows, size_dp, size_tensor, capacity = route_info
    owners = size_dp * size_tensor
    width_model = grad_tokens.shape[1]
    outgoing = (
        jnp.zeros((owners * capacity, width_model), jnp.float32)
        .at[slot_of]
        .set(grad_tokens, mode="drop")
    )
    arrived = lax.all_to_all(
        lax.all_to_all(
            outgoing.reshape(size_dp, size_tensor, capacity, width_model).astype(jnp.bfloat16),
            "dp",
            split_axis=0,
            concat_axis=0,
            tiled=True,
        ),
        "tensor",
        split_axis=1,
        concat_axis=1,
        tiled=True,
    ).astype(jnp.float32)
    arrived = arrived.reshape(owners * capacity, width_model)
    target_rows = jnp.where(found_rows, wanted, shard_rows)
    summed = (
        jnp.zeros((shard_rows, width_model), jnp.float32).at[target_rows].add(arrived, mode="drop")
    )
    counted = (
        jnp.zeros((shard_rows,), jnp.float32)
        .at[target_rows]
        .add(jnp.ones(target_rows.shape, jnp.float32), mode="drop")
    )
    return summed / jnp.maximum(counted, 1.0)[:, None]


def on_device(
    src_ids,
    tgt_ids,
    src_segs,
    tgt_segs,
    embed_table,
    norm_gains,
    enc_qkv,
    enc_out,
    enc_up,
    enc_down,
    dec_qkv,
    dec_out,
    cross_q,
    cross_kv,
    cross_out,
    dec_up,
    dec_down,
    cotangent,
):
    places = Places()
    local_len = src_ids.shape[0]
    width_model = embed_table.shape[1]
    moved = places.swap(
        jnp.concatenate([src_ids.reshape(-1), tgt_ids.reshape(-1), src_segs.reshape(-1), tgt_segs.reshape(-1)])
    )
    src_ids, tgt_ids = moved[:local_len], moved[local_len : 2 * local_len]
    src_row, tgt_row = jnp.split(moved[2 * local_len :], 2)
    offset = (places.core * places.group + places.place) * local_len
    src_live = lax.dynamic_slice_in_dim(src_row, offset, local_len, 0) >= 0
    tgt_live = lax.dynamic_slice_in_dim(tgt_row, offset, local_len, 0) >= 0
    enc_marks = places.marks(src_row, src_row)
    dec_marks = places.marks(tgt_row, tgt_row)
    cross_marks = places.marks(tgt_row, src_row)
    cotangent = places.swap(cotangent.reshape(local_len, width_model))

    shard = enc_qkv.shape[2]
    hidden_shard = enc_up.shape[1]
    narrow = [enc_qkv.reshape(-1, shard), dec_qkv.reshape(-1, shard), cross_q, cross_kv.reshape(-1, shard)]
    narrow_other = places.partner_weight(jnp.concatenate(narrow)).reshape(-1, width_model, shard)
    narrow_own = jnp.concatenate([enc_qkv, dec_qkv, cross_q[None], cross_kv])
    count = narrow_own.shape[0]
    wide = [jnp.concatenate([narrow_own[i], narrow_other[i]], axis=1) for i in range(count)]
    enc_qkv_both, dec_qkv_both, cross_q_both, cross_kv_both = wide[:3], wide[3:6], wide[6], wide[7:9]
    outs_other = places.partner_weight(jnp.concatenate([enc_out, dec_out, cross_out])).reshape(3, shard, -1)
    enc_out_both, dec_out_both, cross_out_both = [
        jnp.concatenate([own, outs_other[i]]) for i, own in enumerate([enc_out, dec_out, cross_out])
    ]
    enc_up_other = places.partner_weight(enc_up)
    enc_down_other = places.partner_weight(enc_down)
    dec_up_other = places.partner_weight(dec_up)
    dec_down_other = places.partner_weight(dec_down)
    enc_ups, enc_downs = [enc_up, enc_up_other], [enc_down, enc_down_other]
    dec_ups, dec_downs = [dec_up, dec_up_other], [dec_down, dec_down_other]

    fetched, route_info = table_lookup(src_ids, tgt_ids, src_live, tgt_live, embed_table)
    src_rows, tgt_rows = fetched[:local_len], fetched[local_len:]
    hidden, src_back = jax.vjp(embed_norm, src_rows, norm_gains[0])
    hidden, enc_attn = attention_forward(
        places, hidden, norm_gains[1], enc_qkv_both, enc_out_both, enc_marks, False
    )
    hidden, enc_ffn = ffn_forward(places, hidden, norm_gains[2], enc_ups, enc_downs)
    memory, memory_back = jax.vjp(layer_norm, hidden, norm_gains[3])
    memory_full = places.gather(memory.astype(BF16))
    state, tgt_back = jax.vjp(embed_norm, tgt_rows, norm_gains[4])
    state, dec_attn = attention_forward(
        places, state, norm_gains[5], dec_qkv_both, dec_out_both, dec_marks, True
    )
    state, dec_cross = cross_forward(
        places, state, norm_gains[6], memory_full, cross_q_both, cross_kv_both, cross_out_both, cross_marks
    )
    state, dec_ffn = ffn_forward(places, state, norm_gains[7], dec_ups, dec_downs)
    final_norm, final_back = jax.vjp(layer_norm, state, norm_gains[8])
    live_target = tgt_live[:, None].astype(F32)
    decoded = places.swap(final_norm * live_target)

    grad_state, gain_final = final_back(cotangent * live_target)
    grad_state, gain_dffn, dec_up_grad, dec_down_grad = ffn_backward(
        places, grad_state, dec_ffn, dec_ups, dec_downs
    )
    grad_state, gain_cross, grad_memory, cross_q_grad, cross_kv_grad, cross_out_grad = cross_backward(
        places, grad_state, dec_cross, memory_full, cross_q_both, cross_kv_both, cross_out_both, cross_marks
    )
    grad_state, gain_dattn, dec_qkv_grad, dec_out_grad = attention_backward(
        places, grad_state, dec_attn, dec_qkv_both, dec_out_both, dec_marks, True
    )
    grad_tgt_rows, gain_demb = tgt_back(grad_state)
    grad_hidden, gain_memory = memory_back(grad_memory)
    grad_hidden, gain_effn, enc_up_grad, enc_down_grad = ffn_backward(
        places, grad_hidden, enc_ffn, enc_ups, enc_downs
    )
    grad_hidden, gain_eattn, enc_qkv_grad, enc_out_grad = attention_backward(
        places, grad_hidden, enc_attn, enc_qkv_both, enc_out_both, enc_marks, False
    )
    grad_src_rows, gain_eemb = src_back(grad_hidden)
    grad_tokens = jnp.concatenate([grad_src_rows, grad_tgt_rows])
    table_grad = table_gradient(grad_tokens, route_info, embed_table.shape[0])
    gain_parts = jnp.stack(
        [
            gain_eemb,
            gain_eattn,
            gain_effn,
            gain_memory,
            gain_demb,
            gain_dattn,
            gain_cross,
            gain_dffn,
            gain_final,
        ]
    )
    gain_grad = lax.psum(gain_parts, ("dp", "tensor"))

    def narrow_sum(grads):
        grads = jnp.stack(grads)
        return places.sum_weight(grads[..., :shard], grads[..., shard:], 1)

    def out_sum(grad):
        return places.sum_weight(grad[:shard], grad[shard:], 1)

    return (
        decoded[:, None],
        table_grad,
        gain_grad,
        narrow_sum(enc_qkv_grad),
        out_sum(enc_out_grad),
        places.sum_weight(*enc_up_grad, 0),
        places.sum_weight(*enc_down_grad, 1),
        narrow_sum(dec_qkv_grad),
        out_sum(dec_out_grad),
        narrow_sum([cross_q_grad])[0],
        narrow_sum(cross_kv_grad),
        out_sum(cross_out_grad),
        places.sum_weight(*dec_up_grad, 0),
        places.sum_weight(*dec_down_grad, 1),
    )


def solution(mesh):
    return jax.shard_map(
        on_device,
        mesh=mesh,
        in_specs=(
            P("tensor", "dp"),
            P("tensor", "dp"),
            P(None, "dp"),
            P(None, "dp"),
            P(("dp", "tensor"), None),
            P(),
            P(None, None, "tensor"),
            P("tensor", None),
            P(None, "tensor"),
            P("tensor", None),
            P(None, None, "tensor"),
            P("tensor", None),
            P(None, "tensor"),
            P(None, None, "tensor"),
            P("tensor", None),
            P(None, "tensor"),
            P("tensor", None),
            P("tensor", "dp", None),
        ),
        out_specs=(
            P("tensor", "dp", None),
            P(("dp", "tensor"), None),
            P(),
            P(None, "dp", "tensor"),
            P("tensor", "dp"),
            P("dp", "tensor"),
            P("tensor", "dp"),
            P(None, "dp", "tensor"),
            P("tensor", "dp"),
            P("dp", "tensor"),
            P(None, "dp", "tensor"),
            P("tensor", "dp"),
            P("dp", "tensor"),
            P("tensor", "dp"),
        ),
        check_vma=False,
    )
```

```python
import math
from functools import partial

import jax
import jax.numpy as jnp
from jax import lax
from jax.experimental import pallas as pl
from jax.experimental.pallas import tpu as pltpu
from jax.sharding import PartitionSpec as P

HEAD_DIM = 64
FACTOR = 0.125

NORM_EPS = 1e-05
MASKED = -1e30
SEGMENTS = 8
F32 = jnp.float32
BF16 = jnp.bfloat16
VMEM_LIMIT = 48 << 20

NN = ((1,), (0,))
NT = ((1,), (1,))
TN = ((0,), (0,))


def dot(lhs, rhs, dims):
    return lax.dot_general(lhs, rhs, (dims, ((), ())), preferred_element_type=F32)


def call(kernel, name, outs, args, grid=(), in_specs=None, out_specs=None, scratch=(), flops=0, exps=0):
    out_shape = [jax.ShapeDtypeStruct(shape, dtype) for shape, dtype in outs]
    moved = sum(math.prod(a.shape) * a.dtype.itemsize for a in list(args) + out_shape)
    specs = {}
    if in_specs is not None:
        specs = dict(in_specs=in_specs, out_specs=out_specs)
    return pl.pallas_call(
        kernel,
        grid=grid,
        out_shape=out_shape,
        scratch_shapes=list(scratch),
        compiler_params=pltpu.CompilerParams(vmem_limit_bytes=VMEM_LIMIT),
        cost_estimate=pl.CostEstimate(flops=flops, transcendentals=exps, bytes_accessed=moved),
        name=name,
        **specs,
    )(*args)


def normal_form(values):
    shifted = values - jnp.mean(values, axis=-1, keepdims=True)
    scale = lax.rsqrt(jnp.mean(shifted * shifted, axis=-1, keepdims=True) + NORM_EPS)
    return shifted * scale, scale


def norm_grad(values, gain, grad):
    normed, scale = normal_form(values)
    inner = grad * gain
    drop = jnp.mean(inner, axis=-1, keepdims=True) + normed * jnp.mean(inner * normed, axis=-1, keepdims=True)
    return scale * (inner - drop), jnp.sum(grad * normed, axis=0, keepdims=True)


def sum_parts(refs):
    total = refs[0][...].astype(F32)
    for ref in refs[1:]:
        total = total + ref[...].astype(F32)
    return total


def fill(refs, value):
    at = 0
    for ref in refs:
        ref[...] = value[at : at + ref.shape[0]].astype(ref.dtype)
        at += ref.shape[0]


def load(refs, scratch):
    at = 0
    for ref in refs:
        scratch[at : at + ref.shape[0]] = ref[...]
        at += ref.shape[0]


def piece_outs(state, count):
    return [((state.shape[0] // count, state.shape[1]), BF16)] * count


def embed_kernel(picks_ref, replies_ref, gains_ref, e_ref, h_ref, t_ref, *out_refs, root):
    length = h_ref.shape[0]
    rows = dot(picks_ref[...], replies_ref[...], TN)
    e_ref[...] = rows.astype(BF16)
    for start, first, state_ref, outs in ((0, 0, h_ref, out_refs[:-1]), (length, 4, t_ref, out_refs[-1:])):
        state = normal_form(rows[start : start + length] * root)[0] * gains_ref[first : first + 1, :]
        state_ref[...] = state
        fill(outs, normal_form(state)[0] * gains_ref[first + 1 : first + 2, :])


def sum_norm_kernel(state_ref, gains_ref, *refs, index, group):
    state = state_ref[...] + sum_parts(refs[:group])
    refs[group][...] = state
    fill(refs[group + 1 :], normal_form(state)[0] * gains_ref[index : index + 1, :])


def sum_norm(state, parts, gains, index, count):
    new, *pieces = call(
        partial(sum_norm_kernel, index=index, group=len(parts)), "sum_norm",
        [(state.shape, F32)] + piece_outs(state, count), [state, gains, *parts], flops=12 * state.size,
    )
    return new, pieces


def final_kernel(state_ref, gains_ref, live_ref, cot_ref, *refs, index, group):
    state = state_ref[...] + sum_parts(refs[:group])
    dec_ref, grad_ref, dg_ref, *outs = refs[group:]
    gain = gains_ref[index : index + 1, :]
    live = live_ref[...]
    dec_ref[...] = (normal_form(state)[0] * gain * live).astype(BF16)
    grad, dg_ref[...] = norm_grad(state, gain, cot_ref[...].astype(F32) * live)
    grad_ref[...] = grad
    fill(outs, grad)


def final(state, parts, gains, live, cotangent, index, count):
    decoded, grad, gain_grad, *pieces = call(
        partial(final_kernel, index=index, group=len(parts)), "final",
        [(state.shape, BF16), (state.shape, F32), ((1, state.shape[1]), F32)] + piece_outs(state, count),
        [state, gains, live, cotangent, *parts], flops=40 * state.size,
    )
    return decoded, grad, pieces, gain_grad


def norm_back_kernel(state_ref, gains_ref, *refs, index, group, adds):
    grad, dg = norm_grad(state_ref[...], gains_ref[index : index + 1, :], sum_parts(refs[:group]))
    refs = refs[group:]
    if adds:
        grad = grad + refs[0][...]
        refs = refs[1:]
    refs[0][...] = grad
    refs[1][...] = dg
    fill(refs[2:], grad)


def norm_back(grad, parts, state, gains, index, count):
    new, gain_grad, *pieces = call(
        partial(norm_back_kernel, index=index, group=len(parts), adds=grad is not None), "norm_back",
        [(state.shape, F32), ((1, state.shape[1]), F32)] + piece_outs(state, count),
        [far(state), gains, *parts] + ([] if grad is None else [grad]), flops=20 * state.size,
    )
    return new, pieces, gain_grad


def embed_back_kernel(grad_ref, state_ref, rows_ref, gains_ref, *refs, index, root, group):
    e_ref, dg_ref, de_ref = refs[group:]
    grad, dg_ref[...] = norm_grad(state_ref[...], gains_ref[index + 1 : index + 2, :], sum_parts(refs[:group]))
    rows = rows_ref[...].astype(F32) * root
    grad, de_ref[...] = norm_grad(rows, gains_ref[index : index + 1, :], grad + grad_ref[...])
    e_ref[...] = (grad * root).astype(BF16)


def embed_back(grad, parts, state, rows, gains, index, root):
    width = state.shape[1]
    return call(
        partial(embed_back_kernel, index=index, root=root, group=len(parts)), "embed_back",
        [(state.shape, BF16), ((1, width), F32), ((1, width), F32)], [grad, far(state), far(rows), gains, *parts],
        flops=40 * state.size,
    )


def weight_specs(weights):
    operands, specs = [], []
    for weight in weights:
        for array, block, index in weight:
            operands.append(far(array))
            specs.append(pl.BlockSpec(block, lambda *_, index=index: index))
    return operands, specs


def flat(ref):
    return ref[...].reshape(-1, ref.shape[-1])


def after(value, *others):
    return lax.optimization_barrier((value, *others))[0]


def far(values):
    return jax.tree.map(lambda value: pltpu.with_memory_space_constraint(value, pltpu.HBM), values)


def whole(array):
    return pl.BlockSpec(array.shape, lambda *_, rank=len(array.shape): (0,) * rank)


def pair_cols(own_ref, other_ref):
    return jnp.concatenate([flat(own_ref), flat(other_ref)], axis=1)


def project_kernel(*refs, pieces, count, scaled):
    x_ref = refs[-1]
    load(refs[:pieces], x_ref)
    refs = refs[pieces:-1]
    values = x_ref[...]
    for i in range(count):
        made = dot(values, pair_cols(refs[2 * i], refs[2 * i + 1]), NN).astype(BF16)
        if scaled and i == 0:
            refs[2 * count][...] = made * jnp.asarray(FACTOR, BF16)
        else:
            out_ref = refs[-1]
            at = (i - int(scaled)) * made.shape[1]
            out_ref[:, at : at + made.shape[1]] = made


def rows_of(pieces):
    return sum(piece.shape[0] for piece in pieces), pieces[0].shape[1]


def project(pieces, weights, shard, scaled):
    length, width = rows_of(pieces)
    operands, specs = weight_specs(weights)
    others = len(weights) - int(scaled)
    outs = [((length, 2 * shard), BF16)] * int(scaled) + [((length, 2 * shard * others), BF16)] * int(others > 0)
    return call(
        partial(project_kernel, pieces=len(pieces), count=len(weights), scaled=scaled), "project", outs,
        [*pieces, *operands], grid=(1,), in_specs=[whole(piece) for piece in pieces] + specs,
        out_specs=[pl.BlockSpec(shape, lambda *_: (0, 0)) for shape, _ in outs],
        scratch=[pltpu.VMEM((length, width), BF16)], flops=4 * length * width * shard * len(weights),
    )


def block_outs(length, width, group):
    shape = (length // group, width)
    return [(shape, BF16)] * group, [pl.BlockSpec(shape, lambda *_: (0, 0))] * group


def unproject_kernel(x_ref, own_ref, other_ref, *out_refs):
    fill(out_refs, dot(x_ref[...], pair_cols(own_ref, other_ref), NT))


def unproject(values, weight, width, group):
    operands, specs = weight_specs([weight])
    outs, out_specs = block_outs(values.shape[0], width, group)
    return call(
        unproject_kernel, "unproject", outs, [values] + operands, grid=(1,), in_specs=[whole(values)] + specs,
        out_specs=out_specs, flops=2 * values.size * width,
    )


def unproject_keys_kernel(*refs, lead, group):
    if lead:
        dq_ref, refs = refs[0], refs[1:]
    mine_ref, theirs_ref = refs[0], refs[1]
    weights, sum_ref, out_refs = refs[2 : -group - 1], refs[-group - 1], refs[-group:]
    summed = (mine_ref[...] + theirs_ref[...].astype(F32)).astype(BF16)
    sum_ref[...] = summed
    span = summed.shape[1] // 2
    total = dot(summed[:, :span], pair_cols(*weights[-4:-2]), NT) + dot(summed[:, span:], pair_cols(*weights[-2:]), NT)
    if lead:
        total = total + dot(dq_ref[...], pair_cols(*weights[:2]), NT)
    fill(out_refs, total)


def unproject_keys(queries_grad, mine, theirs, weights, width, group):
    lead = queries_grad is not None
    operands, specs = weight_specs(weights)
    values = ([queries_grad] if lead else []) + [mine, theirs]
    outs, out_specs = block_outs(mine.shape[0], width, group)
    summed, *parts = call(
        partial(unproject_keys_kernel, lead=lead, group=group), "unproject_keys", [(theirs.shape, BF16)] + outs,
        values + operands, grid=(1,), in_specs=[whole(v) for v in values] + specs, out_specs=[whole(theirs)] + out_specs,
        flops=2 * mine.size * width * len(weights) // 2,
    )
    return parts, summed


def mask_block(sq_ref, sk_ref, pq_ref, base_ref, causal):
    seen = dot(sk_ref[...], sq_ref[...], TN)
    if causal:
        blocks = base_ref.shape[0]
        size = seen.shape[0] // blocks
        index = lax.broadcasted_iota(jnp.int32, (size, seen.shape[1]), 0)
        passed = pq_ref[...]
        seen = jnp.concatenate(
            [
                jnp.where(passed >= index + base_ref[b : b + 1, :], seen[b * size : (b + 1) * size], 0.0)
                for b in range(blocks)
            ]
        )
    return (1.0 - seen) * MASKED


def gather_keys(kv_ref, mine_ref, theirs_ref):
    half = mine_ref.shape[0]
    kv_ref[:half] = mine_ref[...]
    kv_ref[half:] = theirs_ref[...]


def attend_kernel(
    q_ref, mine_ref, theirs_ref, wo_ref, wo2_ref, sq_ref, sk_ref, pq_ref, pk_ref, o_ref, st_ref, *refs, causal, heads
):
    part_refs, kv_ref, part_ref = refs[:-2], refs[-2], refs[-1]

    @pl.when(pl.program_id(0) == 0)
    def _():
        gather_keys(kv_ref, mine_ref, theirs_ref)

    width = heads * HEAD_DIM
    hidden = mask_block(sq_ref, sk_ref, pq_ref, pk_ref, causal)
    for head in range(heads):
        lo, hi = head * HEAD_DIM, (head + 1) * HEAD_DIM
        scores = dot(kv_ref[:, lo:hi], q_ref[:, lo:hi], NT) + hidden
        peak = jnp.max(scores, axis=0, keepdims=True)
        raised = jnp.exp(scores - peak)
        inverse = 1.0 / jnp.sum(raised, axis=0, keepdims=True)
        probs = (raised * inverse).astype(BF16)
        mixed = dot(kv_ref[:, width + lo : width + hi], probs, TN)
        o_ref[:, lo:hi] = mixed.T.astype(BF16)
        st_ref[head : head + 1, :] = peak
        st_ref[heads + head : heads + head + 1, :] = inverse
    half = width // 2
    part = dot(o_ref[:, :half], flat(wo_ref), NN) + dot(o_ref[:, half:], flat(wo2_ref), NN)
    step = part.shape[0]
    part_ref[pl.ds(pl.program_id(0) * step, step)] = part.astype(BF16)

    @pl.when(pl.program_id(0) == pl.num_programs(0) - 1)
    def _():
        fill(part_refs, part_ref)


def mask_specs(step, keys_len, blocks):
    return [
        pl.BlockSpec((SEGMENTS, step), lambda i: (0, i)),
        pl.BlockSpec((SEGMENTS, keys_len), lambda i: (0, 0)),
        pl.BlockSpec((1, step), lambda i: (0, i)),
        pl.BlockSpec((blocks, step), lambda i: (0, 0)),
    ]


def attend(queries, mine, theirs, out_weight, marks, causal, model, group):
    length, width = queries.shape
    keys_len = 2 * length
    heads = width // HEAD_DIM
    step = min(256, length)
    rows = pl.BlockSpec((step, width), lambda i: (i, 0))
    operands, specs = weight_specs([out_weight])
    outs, out_specs = block_outs(length, model, group)
    mixed, stats, *parts = call(
        partial(attend_kernel, causal=causal, heads=heads), "attend",
        [((length, width), BF16), ((2 * heads, length), F32)] + outs,
        [queries, mine, theirs] + operands + list(marks), grid=(length // step,),
        in_specs=[rows, whole(mine), whole(theirs)] + specs + mask_specs(step, keys_len, marks[3].shape[0]),
        out_specs=[rows, pl.BlockSpec((2 * heads, step), lambda i: (0, i))] + out_specs,
        scratch=[pltpu.VMEM((keys_len, 2 * width), BF16), pltpu.VMEM((length, model), BF16)],
        flops=4 * length * keys_len * width, exps=length * keys_len * heads,
    )
    return parts, mixed, stats


def attend_back_kernel(
    wo_ref, wo2_ref, q_ref, mine_ref, theirs_ref, sq_ref, sk_ref, pq_ref, pk_ref, st_ref, *refs, causal, heads
):
    pieces, (dq_ref, dmine_ref, dtheirs_ref, kv_ref, dkv_ref, do_ref, g_ref) = refs[:-7], refs[-7:]
    width = heads * HEAD_DIM
    half = width // 2
    step = dq_ref.shape[0]

    @pl.when(pl.program_id(0) == 0)
    def _():
        gather_keys(kv_ref, mine_ref, theirs_ref)
        dkv_ref[...] = jnp.zeros_like(dkv_ref)
        load(pieces, g_ref)

    grad = g_ref[pl.ds(pl.program_id(0) * step, step)]
    do_ref[:, :half] = dot(grad, flat(wo_ref), NT).astype(BF16)
    do_ref[:, half:] = dot(grad, flat(wo2_ref), NT).astype(BF16)
    hidden = mask_block(sq_ref, sk_ref, pq_ref, pk_ref, causal)
    for head in range(heads):
        lo, hi = head * HEAD_DIM, (head + 1) * HEAD_DIM
        queries, grads = q_ref[:, lo:hi], do_ref[:, lo:hi]
        keys, values = kv_ref[:, lo:hi], kv_ref[:, width + lo : width + hi]
        scores = dot(keys, queries, NT) + hidden
        probs = jnp.exp(scores - st_ref[head : head + 1, :]) * st_ref[heads + head : heads + head + 1, :]
        grad_probs = dot(values, grads, NT)
        inner = jnp.sum(probs * grad_probs, axis=0, keepdims=True)
        grad_scores = (probs * (grad_probs - inner)).astype(BF16)
        dq_ref[:, lo:hi] = (dot(keys, grad_scores, TN) * FACTOR).T.astype(BF16)
        dkv_ref[:, lo:hi] += dot(grad_scores, queries, NN)
        dkv_ref[:, width + lo : width + hi] += dot(probs.astype(BF16), grads, NN)

    @pl.when(pl.program_id(0) == pl.num_programs(0) - 1)
    def _():
        keys_half = dmine_ref.shape[0]
        dmine_ref[...] = dkv_ref[:keys_half]
        dtheirs_ref[...] = dkv_ref[keys_half:].astype(BF16)


def attend_back(pieces, out_weight, queries, mine, theirs, marks, stats, causal):
    length, width = queries.shape
    model = pieces[0].shape[1]
    keys_len = 2 * length
    heads = width // HEAD_DIM
    step = min(256, length)
    rows = pl.BlockSpec((step, width), lambda i: (i, 0))
    operands, specs = weight_specs([out_weight])
    return call(
        partial(attend_back_kernel, causal=causal, heads=heads), "attend_back",
        [((length, width), BF16), ((length, 2 * width), F32), ((length, 2 * width), BF16)],
        operands + far([queries, mine, theirs, *marks, stats]) + [*pieces], grid=(length // step,),
        in_specs=specs
        + [rows, whole(mine), whole(theirs)]
        + mask_specs(step, keys_len, marks[3].shape[0])
        + [pl.BlockSpec((2 * heads, step), lambda i: (0, i))]
        + [whole(piece) for piece in pieces],
        out_specs=[rows, whole(mine), whole(mine)],
        scratch=[
            pltpu.VMEM((keys_len, 2 * width), BF16),
            pltpu.VMEM((keys_len, 2 * width), F32),
            pltpu.VMEM((step, width), BF16),
            pltpu.VMEM((length, model), BF16),
        ],
        flops=10 * length * keys_len * width, exps=length * keys_len * heads,
    )


def attend_grads_kernel(*refs, pieces):
    sources, (dq_ref, dkv_ref, o_ref, out_ref), scratch = refs[:-7], refs[-7:-3], refs[-3:]
    for i, count in enumerate(pieces):
        load(sources[:count], scratch[i])
        sources = sources[count:]
    xq_ref, g_ref = scratch[0], scratch[1]
    xkv_ref = scratch[2] if len(pieces) > 2 else xq_ref
    shard = out_ref.shape[2]
    for index, (cols_ref, at, rhs_ref) in enumerate(
        ((dq_ref, 0, xq_ref), (dkv_ref, 0, xkv_ref), (dkv_ref, 2 * shard, xkv_ref), (o_ref, 0, g_ref))
    ):
        both = dot(cols_ref[:, at : at + 2 * shard], rhs_ref[...], TN).astype(BF16)
        out_ref[0, index] = both[:shard]
        out_ref[1, index] = both[shard:]


def attend_grads(grad_q, grad_kv, mixed, *sources):
    length, model = rows_of(sources[0])
    shard = mixed.shape[1] // 2
    return call(
        partial(attend_grads_kernel, pieces=[len(source) for source in sources]), "attend_grads",
        [((2, 4, shard, model), BF16)], [piece for source in sources for piece in source] + [grad_q, grad_kv, far(mixed)],
        scratch=[pltpu.VMEM((length, model), BF16)] * 3, flops=16 * length * model * shard,
    )[0]


def gelu_pair(pre_act):
    phi_big = 0.5 * (1.0 + lax.erf(pre_act * (1.0 / math.sqrt(2.0))))
    phi_small = jnp.exp(-0.5 * pre_act * pre_act) * (1.0 / math.sqrt(2.0 * math.pi))
    return pre_act * phi_big, phi_big + pre_act * phi_small


def ffn_step(total, acc_ref, out_refs):
    step = pl.program_id(0)

    @pl.when(step == 0)
    def _():
        acc_ref[...] = total

    @pl.when(step > 0)
    def _():
        acc_ref[...] += total

    @pl.when(step == pl.num_programs(0) - 1)
    def _():
        fill(out_refs, acc_ref)


def ffn_kernel(up_ref, up2_ref, dn_ref, dn2_ref, *refs, pieces):
    sources, (act_ref, slope_ref), out_refs, (acc_ref, x_ref) = refs[:pieces], refs[pieces : pieces + 2], refs[pieces + 2 : -2], refs[-2:]

    @pl.when(pl.program_id(0) == 0)
    def _():
        load(sources, x_ref)

    total = None
    for side, (up, down) in enumerate(((up_ref, dn_ref), (up2_ref, dn2_ref))):
        act, slope = gelu_pair(dot(x_ref[...], up[...], NN))
        act = act.astype(BF16)
        act_ref[side] = act
        slope_ref[side] = slope
        term = dot(act, flat(down), NN)
        total = term if total is None else total + term
    ffn_step(total, acc_ref, out_refs)


def ffn_specs(pieces, ups, downs):
    length, model = rows_of(pieces)
    hidden = ups[0].shape[1]
    step = min(256, hidden)
    cols = pl.BlockSpec((model, step), lambda i: (0, i))
    rows = pl.BlockSpec((step, model), lambda i: (i, 0))
    other_rows = rows
    if downs[1].ndim == 3:
        share = hidden // downs[1].shape[0]
        other_rows = pl.BlockSpec((step // share, share, model), lambda i: (i, 0, 0))
    made = pl.BlockSpec((2, length, step), lambda i: (0, 0, i))
    scratch = [pltpu.VMEM((length, model), F32), pltpu.VMEM((length, model), BF16)]
    return length, model, hidden, step, [cols, cols, rows, other_rows], made, [whole(piece) for piece in pieces], scratch


def ffn(pieces, ups, downs, group):
    length, model, hidden, step, specs, made, piece_specs, scratch = ffn_specs(pieces, ups, downs)
    outs, out_specs = block_outs(length, model, group)
    acts, slopes, *parts = call(
        partial(ffn_kernel, pieces=len(pieces)), "ffn",
        [((2, length, hidden), BF16), ((2, length, hidden), F32)] + outs,
        [*far(ups), *far(downs), *pieces], grid=(hidden // step,), in_specs=specs + piece_specs,
        out_specs=[made, made] + out_specs, scratch=scratch, flops=8 * length * model * hidden, exps=4 * length * hidden,
    )
    return parts, acts, slopes


def ffn_back_kernel(up_ref, up2_ref, dn_ref, dn2_ref, slope_ref, *refs, pieces):
    sources, dz_ref, out_refs, (acc_ref, g_ref) = refs[:pieces], refs[pieces], refs[pieces + 1 : -2], refs[-2:]

    @pl.when(pl.program_id(0) == 0)
    def _():
        load(sources, g_ref)

    total = None
    for side, (up, down) in enumerate(((up_ref, dn_ref), (up2_ref, dn2_ref))):
        grad_pre = (slope_ref[side] * dot(g_ref[...], flat(down), NT)).astype(BF16)
        dz_ref[side] = grad_pre
        term = dot(grad_pre, up[...], NT)
        total = term if total is None else total + term
    ffn_step(total, acc_ref, out_refs)


def ffn_back(pieces, ups, downs, slopes, group):
    length, model, hidden, step, specs, made, piece_specs, scratch = ffn_specs(pieces, ups, downs)
    outs, out_specs = block_outs(length, model, group)
    grad_pre, *parts = call(
        partial(ffn_back_kernel, pieces=len(pieces)), "ffn_back", [((2, length, hidden), BF16)] + outs,
        [*far(ups), *far(downs), far(slopes), *pieces], grid=(hidden // step,), in_specs=specs + [made] + piece_specs,
        out_specs=[made] + out_specs, scratch=scratch, flops=8 * length * model * hidden,
    )
    return parts, grad_pre


def ffn_grads_kernel(dz_ref, act_ref, *refs):
    sources, (out_ref, x_ref, g_ref) = refs[:-3], refs[-3:]

    @pl.when((pl.program_id(0) == 0) & (pl.program_id(1) == 0))
    def _():
        load(sources[: len(sources) // 2], x_ref)
        load(sources[len(sources) // 2 :], g_ref)

    out_ref[0, 0] = dot(dz_ref[0], x_ref[...], TN).astype(BF16)
    out_ref[0, 1] = dot(act_ref[0], g_ref[...], TN).astype(BF16)


def ffn_grads(pieces, grads, grad_pre, acts):
    length, model = rows_of(pieces)
    hidden = acts.shape[2]
    step = min(256, hidden)
    made = pl.BlockSpec((1, length, step), lambda s, i: (s, 0, i))
    return call(
        ffn_grads_kernel, "ffn_grads", [((2, 2, hidden, model), BF16)], [grad_pre, far(acts), *far(pieces), *grads],
        grid=(2, hidden // step), in_specs=[made, made] + [whole(p) for p in (*pieces, *grads)],
        out_specs=[pl.BlockSpec((1, 2, step, model), lambda s, i: (s, 0, i, 0))],
        scratch=[pltpu.VMEM((length, model), BF16)] * 2, flops=8 * length * model * hidden,
    )[0]


class Places:
    def __init__(self):
        self.dp_size = lax.axis_size("dp")
        self.tensor_size = lax.axis_size("tensor")
        self.group = self.tensor_size // 2
        self.dp_index = lax.axis_index("dp")
        tensor_index = lax.axis_index("tensor")
        self.core = self.dp_index % 2
        self.place = tensor_index % self.group
        self.pieces = 2 if self.group == 4 else 1

    def swap(self, value):
        pairs = []
        for dp_index in range(self.dp_size):
            for tensor_index in range(self.tensor_size):
                pair, core = divmod(dp_index, 2)
                side, place = divmod(tensor_index, self.group)
                pairs.append(
                    (
                        dp_index * self.tensor_size + tensor_index,
                        (2 * pair + side) * self.tensor_size + core * self.group + place,
                    )
                )
        return lax.ppermute(value, ("dp", "tensor"), pairs)

    def other_core(self, value):
        return lax.ppermute(value, "dp", [(d, d ^ 1) for d in range(self.dp_size)])

    def partner(self, value):
        return lax.ppermute(value, "tensor", [(t, t ^ self.group) for t in range(self.tensor_size)])

    def mate(self, value, offset):
        return lax.ppermute(value, "tensor", [(t, t ^ offset) for t in range(self.tensor_size)])

    def gather(self, pieces):
        if self.pieces == 2:
            low, high = pieces
            low_1, high_2 = self.mate(low, 1), self.mate(high, 2)
            high_1, low_2 = self.mate(high, 1), self.mate(low, 2)
            high_3, low_3 = self.mate(high_2, 1), self.mate(low_1, 2)
            return [low, high, low_1, high_1, low_2, high_2, low_3, high_3]
        return list(pieces) + [self.mate(pieces[0], o) for o in range(1, self.group)]

    def gather_beside(self, block):
        return [block] + [self.mate(block, o) for o in range(1, self.group)]

    def scatter(self, parts):
        return [parts[0]] + [self.mate(parts[o], o) for o in range(1, self.group)]

    def share(self, stacked):
        rows = stacked.shape[0] // self.dp_size
        return lax.dynamic_slice_in_dim(stacked, self.dp_index * rows, rows, 0)

    def split(self, weights):
        rows = weights.shape[1] // self.dp_size
        return lax.dynamic_slice_in_dim(weights, self.dp_index * rows, rows, 1)

    def whole(self, share):
        return lax.all_gather(share, "dp", axis=0)

    def whole_rows(self, share):
        return lax.all_gather(share, "dp", axis=0, tiled=True)

    def sum_weights(self, grads):
        shape = grads.shape
        summed = lax.psum_scatter(grads.reshape(-1, shape[-1]), "dp", scatter_dimension=1, tiled=True)
        return summed.reshape(*shape[:-1], -1)

    def sum_weights_now(self, grads):
        if self.dp_size != 4:
            return self.sum_weights(grads)
        width = grads.shape[-1] // 4
        blocks = [grads[..., i * width : (i + 1) * width] for i in range(4)]
        first = self.core == 0

        def pick(if_first, low, high):
            return jnp.where(if_first, low, high)

        kept = jnp.concatenate([pick(first, *blocks[:2]), pick(first, *blocks[2:])], axis=-1)
        sent = jnp.concatenate([pick(first, *blocks[1::-1]), pick(first, *blocks[:1:-1])], axis=-1)
        kept = kept.astype(F32) + self.other_core(sent).astype(F32)
        low, high = kept[..., :width], kept[..., width:]
        first = self.dp_index < 2
        sent = pick(first, high, low).astype(BF16)
        received = lax.ppermute(sent, "dp", [(d, d ^ 2) for d in range(4)])
        return (pick(first, low, high) + received.astype(F32)).astype(BF16)

    def marks(self, seg_row, seg_key_row):
        kinds = jnp.arange(SEGMENTS)[:, None] - 1
        length = seg_row.shape[0] // self.tensor_size
        order = self.place ^ jnp.arange(self.group)
        blocks = jnp.concatenate([self.core * self.group + order, (1 - self.core) * self.group + order])
        own = jnp.take(seg_row.reshape(-1, length), blocks[: self.group], axis=0).reshape(1, -1)
        keys = jnp.take(seg_key_row.reshape(-1, length), blocks, axis=0).reshape(1, -1)
        positions = (blocks[: self.group, None] * length + jnp.arange(length)[None, :]).reshape(1, -1)
        return (
            ((own == kinds) | (own < 0)).astype(BF16),
            (keys == kinds).astype(BF16),
            positions,
            jnp.broadcast_to(blocks[:, None] * length, (blocks.shape[0], own.shape[1])),
        )


def route(places, token_ids, token_live, shard_rows):
    owners = places.dp_size * places.tensor_size
    tokens = token_ids.shape[0]
    capacity = max(2, 3 * tokens // (2 * owners))
    owner = token_ids // shard_rows
    row = token_ids - owner * shard_rows
    earlier = jnp.arange(tokens)[None, :] < jnp.arange(tokens)[:, None]
    same = (owner[:, None] == owner[None, :]) & token_live[None, :] & earlier
    ranking = jnp.sum(same.astype(jnp.int32), axis=1)
    slot = jnp.where(token_live, owner * capacity + ranking, -1)
    picks = jnp.arange(owners * capacity)[:, None] == slot[None, :]
    requests = jnp.sum(jnp.where(picks, row[None, :] + 1, 0), axis=1) - 1
    return picks.astype(BF16), requests.reshape(owners, capacity)


def to_owners(places, rows, capacity):
    owners = places.dp_size * places.tensor_size
    return lax.all_to_all(
        rows.reshape(owners, capacity, -1), ("dp", "tensor"), split_axis=0, concat_axis=0, tiled=True
    )


def send_back_kernel(picks_ref, e_ref, e2_ref, last_ref, *refs):
    gain_refs, out_ref, rows_ref = refs[:-2], refs[-2], refs[-1]
    length = e_ref.shape[0]
    rows_ref[...] = jnp.zeros_like(rows_ref)
    for i, ref in enumerate(gain_refs):
        rows_ref[i : i + 1] = ref[...]
    sent = dot(picks_ref[:, :length], e_ref[...], NN) + dot(picks_ref[:, length:], e2_ref[...], NN)
    out_ref[...] = (sent + dot(last_ref[...], rows_ref[...].astype(BF16), NN)).astype(BF16)


def send_back(picks, src_grad, tgt_grad, gains, capacity):
    owners = picks.shape[0] // capacity
    slots = jnp.arange(owners * (capacity + 1))
    owner, slot = slots // (capacity + 1), slots % (capacity + 1)
    wider = jnp.take(picks, jnp.minimum(owner * capacity + slot, picks.shape[0] - 1), axis=0)
    wider = jnp.where((slot < capacity)[:, None], wider, jnp.zeros_like(wider))
    rows = 16
    last = (slot == capacity)[:, None] & (owner[:, None] == jnp.arange(rows)[None, :])
    return call(
        send_back_kernel, "send_back", [((slots.shape[0], src_grad.shape[1]), BF16)],
        [wider, src_grad, tgt_grad, last.astype(BF16), *gains], scratch=[pltpu.VMEM((rows, src_grad.shape[1]), F32)],
        flops=2 * wider.size * src_grad.shape[1],
    )[0]


def on_device(
    src_ids,
    tgt_ids,
    src_segs,
    tgt_segs,
    embed_table,
    norm_gains,
    enc_qkv,
    enc_out,
    enc_up,
    enc_down,
    dec_qkv,
    dec_out,
    cross_q,
    cross_kv,
    cross_out,
    dec_up,
    dec_down,
    cotangent,
):
    places = Places()
    group = places.group
    local_len = src_ids.shape[0]
    shard_rows, model = embed_table.shape
    root = math.sqrt(model)
    shard = enc_qkv.shape[2]
    count = places.pieces

    tensor_at = lax.axis_index("tensor") * local_len
    rows_here = [src_segs.reshape(-1), tgt_segs.reshape(-1)]
    ids_here = jnp.concatenate([src_ids.reshape(-1), tgt_ids.reshape(-1)])
    live_here = jnp.concatenate([lax.dynamic_slice_in_dim(row, tensor_at, local_len, 0) for row in rows_here]) >= 0
    enc_in_share = places.partner(places.split(enc_qkv))
    requests = route(places, ids_here, live_here, shard_rows)[1]
    capacity = requests.shape[1]
    moved = places.swap(jnp.concatenate([ids_here] + rows_here))
    wanted = lax.all_to_all(requests, ("dp", "tensor"), split_axis=0, concat_axis=0, tiled=True)
    wanted = wanted.reshape(-1, 2, 2, group * capacity).swapaxes(1, 2).reshape(-1)
    wanted = after(wanted, moved, enc_in_share)
    found = wanted >= 0
    picked = jnp.take(embed_table, jnp.maximum(wanted, 0), axis=0)
    replies = to_owners(places, picked, capacity).reshape(picked.shape)
    outs_share = jnp.concatenate([places.share(weight) for weight in (enc_out, dec_out, cross_out)])
    outs_share = places.partner(after(outs_share, picked))
    replies = after(replies, outs_share)
    cross_share = jnp.concatenate([places.split(cross_q[None]), places.split(cross_kv)])

    token_ids = moved[: 2 * local_len]
    src_row, tgt_row = jnp.split(moved[2 * local_len :], 2)
    offset = (places.core * group + places.place) * local_len
    live = [lax.dynamic_slice_in_dim(row, offset, local_len, 0) >= 0 for row in (src_row, tgt_row)]
    picks = route(places, token_ids, jnp.concatenate(live), shard_rows)[0]
    enc_marks = places.marks(src_row, src_row)
    dec_marks = places.marks(tgt_row, tgt_row)
    cross_marks = places.marks(tgt_row, src_row)

    def narrow(own, own_index, other, other_index):
        if own.ndim == 2:
            own_part = (own, own.shape, (0, 0))
        else:
            own_part = (own, (1, *own.shape[1:]), (own_index, 0, 0))
        return own_part, (other, (other.shape[0], 1, *other.shape[2:]), (0, other_index, 0, 0))

    def wide(own, other, index):
        rows = own.shape[0] // places.dp_size
        return (own, own.shape, (0, 0)), (other, (other.shape[0], rows, model), (0, index, 0))

    def narrow_whole(share, start):
        share = after(share, start)
        return places.whole(jnp.concatenate([share, share]))

    enc_in_other = narrow_whole(enc_in_share, picked)
    enc_in = [narrow(enc_qkv, i, enc_in_other, i) for i in range(3)]

    token_shape = (local_len, model)
    embeds, h0, t0, *pieces = call(
        partial(embed_kernel, root=root), "embed",
        [((2 * local_len, model), BF16), (token_shape, F32), (token_shape, F32)] + [((local_len // count, model), BF16)] * count + [(token_shape, BF16)],
        [picks, replies, norm_gains],
    )
    a1, c1 = pieces[:-1], pieces[-1]
    down_rows = enc_down.shape[0] // places.dp_size
    out_rows = shard // places.dp_size
    outs_other = narrow_whole(outs_share, a1)
    dec_in_share = places.partner(after(places.split(dec_qkv), a1))
    a1 = places.gather(a1)
    c1 = places.gather_beside(after(c1, a1))
    out_rows = shard // places.dp_size
    if out_rows % 8:
        outs_other = [outs_other[:, i * out_rows : (i + 1) * out_rows] for i in range(3)]
        enc_o, dec_o, cross_o = [wide(own, other, 0) for own, other in zip((enc_out, dec_out, cross_out), outs_other)]
    else:
        enc_o, dec_o, cross_o = [wide(own, outs_other, i) for i, own in enumerate((enc_out, dec_out, cross_out))]
    enc_q, enc_mine = project(a1, enc_in, shard, True)
    dec_in_other = narrow_whole(dec_in_share, enc_mine)
    dec_in = [narrow(dec_qkv, i, dec_in_other, i) for i in range(3)]
    enc_theirs = places.other_core(enc_mine)
    parts, enc_mixed, enc_stats = attend(enc_q, enc_mine, enc_theirs, enc_o, enc_marks, False, model, group)
    enc_up_share = places.partner(after(places.share(enc_up), enc_mine))
    enc_down_share = places.partner(after(places.share(enc_down), enc_mine))
    own_parts = after(parts, enc_up_share, c1)
    enc_ups = [enc_up, places.whole_rows(after(enc_up_share, own_parts))]
    parts = places.scatter(own_parts)
    dec_q, dec_mine = project(after(c1, own_parts), dec_in, shard, True)
    dec_theirs = places.other_core(dec_mine)
    cross_share = places.partner(after(cross_share, dec_mine))
    cot_moved = places.swap(after(cotangent.reshape(token_shape).astype(BF16), dec_mine))
    dec_parts, dec_mixed, dec_stats = attend(
        after(dec_q, enc_down_share), dec_mine, dec_theirs, dec_o, dec_marks, True, model, group
    )
    enc_downs = [enc_down, places.whole_rows(after(enc_down_share, dec_q))]
    h1, own_b1 = sum_norm(h0, after(parts, dec_parts, cot_moved), norm_gains, 2, count)

    b1 = places.gather(own_b1)
    cross_other = narrow_whole(cross_share, own_b1)
    dec_parts = places.scatter(after(dec_parts, own_b1))
    t1, (own_c2,) = sum_norm(t0, after(dec_parts, b1), norm_gains, 6, 1)
    dec_up_share = places.partner(after(places.share(dec_up), own_c2))
    b1 = after(b1, own_c2)
    c2 = places.gather_beside(own_c2)
    own_parts, enc_acts, enc_slopes = ffn(b1, enc_ups, enc_downs, group)
    own_parts = after(own_parts, c2)
    cross_in = narrow(cross_q, 0, cross_other, 0)
    cross_mem = [narrow(cross_kv, i, cross_other, 1 + i) for i in range(2)]
    parts = places.scatter(own_parts)
    h2, own_memory = sum_norm(h1, parts, norm_gains, 3, count)
    dec_ups = [dec_up, places.whole_rows(after(dec_up_share, own_memory))]
    memory = places.gather(own_memory)
    cross_qs = project(after(c2, own_memory), [cross_in], shard, True)[0]
    cross_mine = project(after(memory, cross_qs), cross_mem, shard, False)[0]
    dec_down_share = places.partner(after(places.share(dec_down), cross_mine))
    cross_theirs = places.other_core(cross_mine)
    parts, cross_mixed, cross_stats = attend(
        cross_qs, cross_mine, cross_theirs, cross_o, cross_marks, False, model, group
    )
    dec_downs = [dec_down, places.whole_rows(after(dec_down_share, parts))]
    t2, own_f1 = sum_norm(t1, places.scatter(parts), norm_gains, 7, count)
    f1 = places.gather(own_f1)
    parts, dec_acts, dec_slopes = ffn(f1, dec_ups, dec_downs, group)
    decoded, grad_t, pieces, gain_final = final(
        t2, places.scatter(parts), norm_gains, live[1][:, None].astype(F32), cot_moved, 8, count
    )

    grad_full = places.gather(pieces)
    decoded = places.swap(after(decoded, grad_full))
    own_parts, grad_pre = ffn_back(grad_full, dec_ups, dec_downs, dec_slopes, group)
    dec_ffn_grads = ffn_grads(f1, after(grad_full, own_parts), grad_pre, dec_acts)
    parts = after(places.scatter(own_parts), dec_ffn_grads)
    grad_t, pieces, gain_dffn = norm_back(grad_t, parts, t2, norm_gains, 7, count)

    dec_ffn_sum = places.sum_weights(after(dec_ffn_grads, pieces))
    grad_full = after(places.gather(pieces), decoded)
    grad_q, mine, theirs = attend_back(
        grad_full, cross_o, cross_qs, cross_mine, cross_theirs, cross_marks, cross_stats, False
    )
    theirs = places.other_core(theirs)
    own_parts = unproject(grad_q, cross_in, model, group)
    own_mem_parts, grad_kv = unproject_keys(None, mine, after(theirs, own_parts), cross_mem, model, group)
    mem_parts = places.scatter(own_mem_parts)
    cross_grads = attend_grads(grad_q, grad_kv, cross_mixed, far(c2), after(grad_full, own_mem_parts), far(memory))
    grad_h, pieces_h, gain_memory = norm_back(None, after(mem_parts, cross_grads), h2, norm_gains, 3, count)
    cross_sum = places.sum_weights(after(cross_grads, pieces_h))

    enc_full = places.gather(pieces_h)
    parts = places.scatter(after(own_parts, enc_full))
    dec_ffn_other = places.partner(after(dec_ffn_sum[1], enc_full))
    own_parts, grad_pre = ffn_back(enc_full, enc_ups, enc_downs, enc_slopes, group)
    h_parts = places.scatter(own_parts)
    enc_ffn_grads = ffn_grads(b1, after(enc_full, own_parts), grad_pre, enc_acts)
    grad_t, pieces, gain_cross = norm_back(grad_t, after(parts, enc_ffn_grads, dec_ffn_sum), t1, norm_gains, 6, count)
    dec_full = places.gather(pieces)
    grad_h, pieces_h, gain_effn = norm_back(grad_h, after(h_parts, pieces), h1, norm_gains, 2, 1)
    hidden_full = places.gather_beside(pieces_h[0])
    dec_full = after(dec_full, pieces_h, dec_ffn_other)
    cross_sum_other = places.partner(after(cross_sum[1], dec_full))
    enc_ffn_sum = places.sum_weights(after(enc_ffn_grads, cross_sum, pieces_h))
    grad_q, mine, theirs = attend_back(dec_full, dec_o, dec_q, dec_mine, dec_theirs, dec_marks, dec_stats, True)
    theirs = places.other_core(theirs)
    own_parts, grad_kv = unproject_keys(grad_q, mine, theirs, dec_in, model, group)
    dec_parts = places.scatter(own_parts)
    dec_grads = attend_grads(grad_q, grad_kv, dec_mixed, far(c1), after(dec_full, own_parts))

    grad_full = after(hidden_full, dec_grads, cross_sum_other)
    enc_ffn_other = places.partner(after(enc_ffn_sum[1], grad_full))
    grad_q, mine, theirs = attend_back(grad_full, enc_o, enc_q, enc_mine, enc_theirs, enc_marks, enc_stats, False)
    theirs = places.other_core(theirs)
    dec_sum = places.sum_weights(after(dec_grads, enc_ffn_sum, grad_full))
    own_parts, grad_kv = unproject_keys(grad_q, mine, theirs, enc_in, model, group)
    parts = places.scatter(after(own_parts, enc_ffn_other))
    tgt_grad, gain_dattn, gain_demb = embed_back(
        grad_t, after(dec_parts, own_parts), t0, embeds[local_len:], norm_gains, 4, root
    )
    src_grad, gain_eattn, gain_eemb = embed_back(
        grad_h, after(parts, tgt_grad), h0, embeds[:local_len], norm_gains, 0, root
    )

    gains = [
        gain_eemb, gain_eattn, gain_effn, gain_memory, gain_demb, gain_dattn, gain_cross, gain_dffn, gain_final
    ]
    outgoing = send_back(picks, src_grad, tgt_grad, gains, capacity)
    arrived = to_owners(places, outgoing, capacity + 1)
    enc_grads = attend_grads(grad_q, grad_kv, enc_mixed, far(a1), after(grad_full, outgoing))
    enc_sum = places.sum_weights_now(enc_grads)
    dec_sum_other = places.partner(after(dec_sum[1], outgoing))
    enc_sum_other = places.partner(enc_sum[1])
    arrived = after(arrived, enc_sum)
    gain_sum = jnp.sum(arrived[:, capacity].astype(F32), axis=0)
    gain_grad = lax.all_to_all(
        jnp.broadcast_to(gain_sum[None], (arrived.shape[0], model)), ("dp", "tensor"), 0, 0, tiled=True
    )[: len(gains)]
    counts = jnp.sum(((wanted[:, None] == wanted[None, :]) & found[None, :]).astype(F32), axis=1)
    rows = arrived[:, :capacity].reshape(-1, model).astype(F32) / jnp.maximum(counts, 1.0)[:, None]
    target_rows = jnp.where(found, wanted, shard_rows)
    table_grad = jnp.zeros((shard_rows, model), F32).at[target_rows].add(rows, mode="drop")

    def finish(summed, other):
        return summed[0].astype(F32) + other.astype(F32)

    dec_ffn_sum = finish(dec_ffn_sum, dec_ffn_other)
    cross_sum = finish(cross_sum, cross_sum_other)
    enc_ffn_sum = finish(enc_ffn_sum, enc_ffn_other)
    dec_sum = finish(dec_sum, dec_sum_other)
    enc_sum = finish(enc_sum, enc_sum_other)

    def turned(grads):
        return jnp.swapaxes(grads, -1, -2)

    return (
        decoded.astype(F32)[:, None],
        table_grad,
        gain_grad,
        turned(enc_sum[:3]),
        enc_sum[3],
        turned(enc_ffn_sum[0]),
        enc_ffn_sum[1],
        turned(dec_sum[:3]),
        dec_sum[3],
        turned(cross_sum[0]),
        turned(cross_sum[1:3]),
        cross_sum[3],
        turned(dec_ffn_sum[0]),
        dec_ffn_sum[1],
    )


def solution(mesh):
    return jax.shard_map(
        on_device,
        mesh=mesh,
        in_specs=(
            P("tensor", "dp"),
            P("tensor", "dp"),
            P(None, "dp"),
            P(None, "dp"),
            P(("dp", "tensor"), None),
            P(),
            P(None, None, "tensor"),
            P("tensor", None),
            P(None, "tensor"),
            P("tensor", None),
            P(None, None, "tensor"),
            P("tensor", None),
            P(None, "tensor"),
            P(None, None, "tensor"),
            P("tensor", None),
            P(None, "tensor"),
            P("tensor", None),
            P("tensor", "dp", None),
        ),
        out_specs=(
            P("tensor", "dp", None),
            P(("dp", "tensor"), None),
            P(),
            P(None, "dp", "tensor"),
            P("tensor", "dp"),
            P("dp", "tensor"),
            P("tensor", "dp"),
            P(None, "dp", "tensor"),
            P("tensor", "dp"),
            P("dp", "tensor"),
            P(None, "dp", "tensor"),
            P("tensor", "dp"),
            P("dp", "tensor"),
            P("tensor", "dp"),
        ),
        check_vma=False,
    )
```

```python
import math
from functools import partial

import jax
import jax.numpy as jnp
from jax import lax
from jax.experimental import pallas as pl
from jax.experimental.pallas import tpu as pltpu
from jax.sharding import PartitionSpec as P

HEAD_DIM = 64
FACTOR = 0.125

NORM_EPS = 1e-05
MASKED = -1e30
SEGMENTS = 8
F32 = jnp.float32
BF16 = jnp.bfloat16
VMEM_LIMIT = 48 << 20

NN = ((1,), (0,))
NT = ((1,), (1,))
TN = ((0,), (0,))


def dot(lhs, rhs, dims):
    return lax.dot_general(lhs, rhs, (dims, ((), ())), preferred_element_type=F32)


def call(kernel, name, outs, args, grid=(), in_specs=None, out_specs=None, scratch=(), flops=0, exps=0):
    out_shape = [jax.ShapeDtypeStruct(shape, dtype) for shape, dtype in outs]
    moved = sum(math.prod(a.shape) * a.dtype.itemsize for a in list(args) + out_shape)
    specs = {}
    if in_specs is not None:
        specs = dict(in_specs=in_specs, out_specs=out_specs)
    return pl.pallas_call(
        kernel,
        grid=grid,
        out_shape=out_shape,
        scratch_shapes=list(scratch),
        compiler_params=pltpu.CompilerParams(vmem_limit_bytes=VMEM_LIMIT),
        cost_estimate=pl.CostEstimate(flops=flops // 50, transcendentals=exps // 50, bytes_accessed=moved // 50),
        name=name,
        **specs,
    )(*args)


def normal_form(values):
    shifted = values - jnp.mean(values, axis=-1, keepdims=True)
    scale = lax.rsqrt(jnp.mean(shifted * shifted, axis=-1, keepdims=True) + NORM_EPS)
    return shifted * scale, scale


def norm_grad(values, gain, grad):
    normed, scale = normal_form(values)
    inner = grad * gain
    drop = jnp.mean(inner, axis=-1, keepdims=True) + normed * jnp.mean(inner * normed, axis=-1, keepdims=True)
    return scale * (inner - drop), jnp.sum(grad * normed, axis=0, keepdims=True)


def sum_parts(refs):
    total = refs[0][...].astype(F32)
    for ref in refs[1:]:
        total = total + ref[...].astype(F32)
    return total


def fill(refs, value):
    at = 0
    for ref in refs:
        ref[...] = value[at : at + ref.shape[0]].astype(ref.dtype)
        at += ref.shape[0]


def load(refs, scratch):
    at = 0
    for ref in refs:
        scratch[at : at + ref.shape[0]] = ref[...]
        at += ref.shape[0]


def piece_outs(state, count):
    return [((state.shape[0] // count, state.shape[1]), BF16)] * count


def embed_kernel(picks_ref, replies_ref, gains_ref, e_ref, h_ref, t_ref, *out_refs, root):
    length = h_ref.shape[0]
    rows = dot(picks_ref[...], replies_ref[...], TN)
    e_ref[...] = rows.astype(BF16)
    for start, first, state_ref, outs in ((0, 0, h_ref, out_refs[:-1]), (length, 4, t_ref, out_refs[-1:])):
        state = normal_form(rows[start : start + length] * root)[0] * gains_ref[first : first + 1, :]
        state_ref[...] = state
        fill(outs, normal_form(state)[0] * gains_ref[first + 1 : first + 2, :])


def sum_norm_kernel(state_ref, gains_ref, *refs, index, group):
    state = state_ref[...] + sum_parts(refs[:group])
    refs[group][...] = state
    fill(refs[group + 1 :], normal_form(state)[0] * gains_ref[index : index + 1, :])


def sum_norm(state, parts, gains, index, count):
    new, *pieces = call(
        partial(sum_norm_kernel, index=index, group=len(parts)), "sum_norm",
        [(state.shape, F32)] + piece_outs(state, count), [state, gains, *parts], flops=12 * state.size,
    )
    return new, pieces


def final_kernel(state_ref, gains_ref, live_ref, cot_ref, *refs, index, group):
    state = state_ref[...] + sum_parts(refs[:group])
    dec_ref, grad_ref, dg_ref, *outs = refs[group:]
    gain = gains_ref[index : index + 1, :]
    live = live_ref[...]
    dec_ref[...] = (normal_form(state)[0] * gain * live).astype(BF16)
    grad, dg_ref[...] = norm_grad(state, gain, cot_ref[...].astype(F32) * live)
    grad_ref[...] = grad
    fill(outs, grad)


def final(state, parts, gains, live, cotangent, index, count):
    decoded, grad, gain_grad, *pieces = call(
        partial(final_kernel, index=index, group=len(parts)), "final",
        [(state.shape, BF16), (state.shape, F32), ((1, state.shape[1]), F32)] + piece_outs(state, count),
        [state, gains, live, cotangent, *parts], flops=40 * state.size,
    )
    return decoded, grad, pieces, gain_grad


def norm_back_kernel(state_ref, gains_ref, *refs, index, group, adds):
    grad, dg = norm_grad(state_ref[...], gains_ref[index : index + 1, :], sum_parts(refs[:group]))
    refs = refs[group:]
    if adds:
        grad = grad + refs[0][...]
        refs = refs[1:]
    refs[0][...] = grad
    refs[1][...] = dg
    fill(refs[2:], grad)


def norm_back(grad, parts, state, gains, index, count):
    new, gain_grad, *pieces = call(
        partial(norm_back_kernel, index=index, group=len(parts), adds=grad is not None), "norm_back",
        [(state.shape, F32), ((1, state.shape[1]), F32)] + piece_outs(state, count),
        [far(state), gains, *parts] + ([] if grad is None else [grad]), flops=20 * state.size,
    )
    return new, pieces, gain_grad


def embed_back_kernel(grad_ref, state_ref, rows_ref, gains_ref, *refs, index, root, group):
    e_ref, dg_ref, de_ref = refs[group:]
    grad, dg_ref[...] = norm_grad(state_ref[...], gains_ref[index + 1 : index + 2, :], sum_parts(refs[:group]))
    rows = rows_ref[...].astype(F32) * root
    grad, de_ref[...] = norm_grad(rows, gains_ref[index : index + 1, :], grad + grad_ref[...])
    e_ref[...] = (grad * root).astype(BF16)


def embed_back(grad, parts, state, rows, gains, index, root):
    width = state.shape[1]
    return call(
        partial(embed_back_kernel, index=index, root=root, group=len(parts)), "embed_back",
        [(state.shape, BF16), ((1, width), F32), ((1, width), F32)], [grad, far(state), far(rows), gains, *parts],
        flops=40 * state.size,
    )


def weight_specs(weights):
    operands, specs = [], []
    for weight in weights:
        for array, block, index in weight:
            operands.append(far(array))
            specs.append(pl.BlockSpec(block, lambda *_, index=index: index))
    return operands, specs


def flat(ref):
    return ref[...].reshape(-1, ref.shape[-1])


def after(value, *others):
    return lax.optimization_barrier((value, *others))[0]


def far(values):
    return jax.tree.map(lambda value: pltpu.with_memory_space_constraint(value, pltpu.HBM), values)


def whole(array):
    return pl.BlockSpec(array.shape, lambda *_, rank=len(array.shape): (0,) * rank)


def pair_cols(own_ref, other_ref):
    return jnp.concatenate([flat(own_ref), flat(other_ref)], axis=1)


def project_kernel(*refs, pieces, count, scaled):
    x_ref = refs[-1]
    load(refs[:pieces], x_ref)
    refs = refs[pieces:-1]
    values = x_ref[...]
    for i in range(count):
        made = dot(values, pair_cols(refs[2 * i], refs[2 * i + 1]), NN).astype(BF16)
        if scaled and i == 0:
            refs[2 * count][...] = made * jnp.asarray(FACTOR, BF16)
        else:
            out_ref = refs[-1]
            at = (i - int(scaled)) * made.shape[1]
            out_ref[:, at : at + made.shape[1]] = made


def rows_of(pieces):
    return sum(piece.shape[0] for piece in pieces), pieces[0].shape[1]


def project(pieces, weights, shard, scaled):
    length, width = rows_of(pieces)
    operands, specs = weight_specs(weights)
    others = len(weights) - int(scaled)
    outs = [((length, 2 * shard), BF16)] * int(scaled) + [((length, 2 * shard * others), BF16)] * int(others > 0)
    return call(
        partial(project_kernel, pieces=len(pieces), count=len(weights), scaled=scaled), "project", outs,
        [*pieces, *operands], grid=(1,), in_specs=[whole(piece) for piece in pieces] + specs,
        out_specs=[pl.BlockSpec(shape, lambda *_: (0, 0)) for shape, _ in outs],
        scratch=[pltpu.VMEM((length, width), BF16)], flops=4 * length * width * shard * len(weights),
    )


def block_outs(length, width, group):
    shape = (length // group, width)
    return [(shape, BF16)] * group, [pl.BlockSpec(shape, lambda *_: (0, 0))] * group


def unproject_kernel(x_ref, own_ref, other_ref, *out_refs):
    fill(out_refs, dot(x_ref[...], pair_cols(own_ref, other_ref), NT))


def unproject(values, weight, width, group):
    operands, specs = weight_specs([weight])
    outs, out_specs = block_outs(values.shape[0], width, group)
    return call(
        unproject_kernel, "unproject", outs, [values] + operands, grid=(1,), in_specs=[whole(values)] + specs,
        out_specs=out_specs, flops=2 * values.size * width,
    )


def unproject_keys_kernel(*refs, lead, group):
    if lead:
        dq_ref, refs = refs[0], refs[1:]
    mine_ref, theirs_ref = refs[0], refs[1]
    weights, sum_ref, out_refs = refs[2 : -group - 1], refs[-group - 1], refs[-group:]
    summed = (mine_ref[...] + theirs_ref[...].astype(F32)).astype(BF16)
    sum_ref[...] = summed
    span = summed.shape[1] // 2
    total = dot(summed[:, :span], pair_cols(*weights[-4:-2]), NT) + dot(summed[:, span:], pair_cols(*weights[-2:]), NT)
    if lead:
        total = total + dot(dq_ref[...], pair_cols(*weights[:2]), NT)
    fill(out_refs, total)


def unproject_keys(queries_grad, mine, theirs, weights, width, group):
    lead = queries_grad is not None
    operands, specs = weight_specs(weights)
    values = ([queries_grad] if lead else []) + [mine, theirs]
    outs, out_specs = block_outs(mine.shape[0], width, group)
    summed, *parts = call(
        partial(unproject_keys_kernel, lead=lead, group=group), "unproject_keys", [(theirs.shape, BF16)] + outs,
        values + operands, grid=(1,), in_specs=[whole(v) for v in values] + specs, out_specs=[whole(theirs)] + out_specs,
        flops=2 * mine.size * width * len(weights) // 2,
    )
    return parts, summed


def mask_block(sq_ref, sk_ref, pq_ref, base_ref, causal):
    seen = dot(sk_ref[...], sq_ref[...], TN)
    if causal:
        blocks = base_ref.shape[0]
        size = seen.shape[0] // blocks
        index = lax.broadcasted_iota(jnp.int32, (size, seen.shape[1]), 0)
        passed = pq_ref[...]
        seen = jnp.concatenate(
            [
                jnp.where(passed >= index + base_ref[b : b + 1, :], seen[b * size : (b + 1) * size], 0.0)
                for b in range(blocks)
            ]
        )
    return (1.0 - seen) * MASKED


def gather_keys(kv_ref, mine_ref, theirs_ref):
    half = mine_ref.shape[0]
    kv_ref[:half] = mine_ref[...]
    kv_ref[half:] = theirs_ref[...]


def attend_kernel(
    q_ref, mine_ref, theirs_ref, wo_ref, wo2_ref, sq_ref, sk_ref, pq_ref, pk_ref, o_ref, st_ref, *refs, causal, heads
):
    part_refs, kv_ref, part_ref = refs[:-2], refs[-2], refs[-1]

    @pl.when(pl.program_id(0) == 0)
    def _():
        gather_keys(kv_ref, mine_ref, theirs_ref)

    width = heads * HEAD_DIM
    hidden = mask_block(sq_ref, sk_ref, pq_ref, pk_ref, causal)
    for head in range(heads):
        lo, hi = head * HEAD_DIM, (head + 1) * HEAD_DIM
        scores = dot(kv_ref[:, lo:hi], q_ref[:, lo:hi], NT) + hidden
        peak = jnp.max(scores, axis=0, keepdims=True)
        raised = jnp.exp(scores - peak)
        summed = jnp.sum(raised, axis=0, keepdims=True)
        mixed = dot(kv_ref[:, width + lo : width + hi], raised.astype(BF16), TN) * (1.0 / summed)
        o_ref[:, lo:hi] = mixed.T.astype(BF16)
        st_ref[head : head + 1, :] = peak + jnp.log(summed)
    half = width // 2
    part = dot(o_ref[:, :half], flat(wo_ref), NN) + dot(o_ref[:, half:], flat(wo2_ref), NN)
    step = part.shape[0]
    part_ref[pl.ds(pl.program_id(0) * step, step)] = part.astype(BF16)

    @pl.when(pl.program_id(0) == pl.num_programs(0) - 1)
    def _():
        fill(part_refs, part_ref)


def mask_specs(step, keys_len, blocks):
    return [
        pl.BlockSpec((SEGMENTS, step), lambda i: (0, i)),
        pl.BlockSpec((SEGMENTS, keys_len), lambda i: (0, 0)),
        pl.BlockSpec((1, step), lambda i: (0, i)),
        pl.BlockSpec((blocks, step), lambda i: (0, 0)),
    ]


def attend(queries, mine, theirs, out_weight, marks, causal, model, group):
    length, width = queries.shape
    keys_len = 2 * length
    heads = width // HEAD_DIM
    step = min(256, length)
    rows = pl.BlockSpec((step, width), lambda i: (i, 0))
    operands, specs = weight_specs([out_weight])
    outs, out_specs = block_outs(length, model, group)
    mixed, stats, *parts = call(
        partial(attend_kernel, causal=causal, heads=heads), "attend",
        [((length, width), BF16), ((heads, length), F32)] + outs,
        [queries, mine, theirs] + operands + list(marks), grid=(length // step,),
        in_specs=[rows, whole(mine), whole(theirs)] + specs + mask_specs(step, keys_len, marks[3].shape[0]),
        out_specs=[rows, pl.BlockSpec((heads, step), lambda i: (0, i))] + out_specs,
        scratch=[pltpu.VMEM((keys_len, 2 * width), BF16), pltpu.VMEM((length, model), BF16)],
        flops=4 * length * keys_len * width, exps=length * keys_len * heads,
    )
    return parts, mixed, stats


def attend_back_kernel(
    wo_ref, wo2_ref, q_ref, mine_ref, theirs_ref, sq_ref, sk_ref, pq_ref, pk_ref, st_ref, *refs, causal, heads
):
    pieces, (dq_ref, dmine_ref, dtheirs_ref, kv_ref, dkv_ref, do_ref, g_ref) = refs[:-7], refs[-7:]
    width = heads * HEAD_DIM
    half = width // 2
    step = dq_ref.shape[0]

    @pl.when(pl.program_id(0) == 0)
    def _():
        gather_keys(kv_ref, mine_ref, theirs_ref)
        dkv_ref[...] = jnp.zeros_like(dkv_ref)
        load(pieces, g_ref)

    grad = g_ref[pl.ds(pl.program_id(0) * step, step)]
    do_ref[:, :half] = dot(grad, flat(wo_ref), NT).astype(BF16)
    do_ref[:, half:] = dot(grad, flat(wo2_ref), NT).astype(BF16)
    hidden = mask_block(sq_ref, sk_ref, pq_ref, pk_ref, causal)
    for head in range(heads):
        lo, hi = head * HEAD_DIM, (head + 1) * HEAD_DIM
        queries, grads = q_ref[:, lo:hi], do_ref[:, lo:hi]
        keys, values = kv_ref[:, lo:hi], kv_ref[:, width + lo : width + hi]
        scores = dot(keys, queries, NT) + hidden
        probs = jnp.exp(scores - st_ref[head : head + 1, :])
        grad_probs = dot(values, grads, NT)
        inner = jnp.sum(probs * grad_probs, axis=0, keepdims=True)
        grad_scores = (probs * (grad_probs - inner)).astype(BF16)
        dq_ref[:, lo:hi] = (dot(keys, grad_scores, TN) * FACTOR).T.astype(BF16)
        dkv_ref[:, lo:hi] += dot(grad_scores, queries, NN)
        dkv_ref[:, width + lo : width + hi] += dot(probs.astype(BF16), grads, NN)

    @pl.when(pl.program_id(0) == pl.num_programs(0) - 1)
    def _():
        keys_half = dmine_ref.shape[0]
        dmine_ref[...] = dkv_ref[:keys_half]
        dtheirs_ref[...] = dkv_ref[keys_half:].astype(BF16)


def attend_back(pieces, out_weight, queries, mine, theirs, marks, stats, causal):
    length, width = queries.shape
    model = pieces[0].shape[1]
    keys_len = 2 * length
    heads = width // HEAD_DIM
    step = min(256, length)
    rows = pl.BlockSpec((step, width), lambda i: (i, 0))
    operands, specs = weight_specs([out_weight])
    return call(
        partial(attend_back_kernel, causal=causal, heads=heads), "attend_back",
        [((length, width), BF16), ((length, 2 * width), F32), ((length, 2 * width), BF16)],
        operands + far([queries, mine, theirs, *marks, stats]) + [*pieces], grid=(length // step,),
        in_specs=specs
        + [rows, whole(mine), whole(theirs)]
        + mask_specs(step, keys_len, marks[3].shape[0])
        + [pl.BlockSpec((heads, step), lambda i: (0, i))]
        + [whole(piece) for piece in pieces],
        out_specs=[rows, whole(mine), whole(mine)],
        scratch=[
            pltpu.VMEM((keys_len, 2 * width), BF16),
            pltpu.VMEM((keys_len, 2 * width), F32),
            pltpu.VMEM((step, width), BF16),
            pltpu.VMEM((length, model), BF16),
        ],
        flops=10 * length * keys_len * width, exps=length * keys_len * heads,
    )


def attend_grads_kernel(*refs, pieces):
    sources, (dq_ref, dkv_ref, o_ref, out_ref), scratch = refs[:-7], refs[-7:-3], refs[-3:]
    for i, count in enumerate(pieces):
        load(sources[:count], scratch[i])
        sources = sources[count:]
    xq_ref, g_ref = scratch[0], scratch[1]
    xkv_ref = scratch[2] if len(pieces) > 2 else xq_ref
    shard = out_ref.shape[2]
    for index, (cols_ref, at, rhs_ref) in enumerate(
        ((dq_ref, 0, xq_ref), (dkv_ref, 0, xkv_ref), (dkv_ref, 2 * shard, xkv_ref), (o_ref, 0, g_ref))
    ):
        both = dot(cols_ref[:, at : at + 2 * shard], rhs_ref[...], TN).astype(BF16)
        out_ref[0, index] = both[:shard]
        out_ref[1, index] = both[shard:]


def attend_grads(grad_q, grad_kv, mixed, *sources):
    length, model = rows_of(sources[0])
    shard = mixed.shape[1] // 2
    return call(
        partial(attend_grads_kernel, pieces=[len(source) for source in sources]), "attend_grads",
        [((2, 4, shard, model), BF16)], [piece for source in sources for piece in source] + [grad_q, grad_kv, far(mixed)],
        scratch=[pltpu.VMEM((length, model), BF16)] * 3, flops=16 * length * model * shard,
    )[0]


def gelu_pair(pre_act):
    phi_big = 0.5 * (1.0 + lax.erf(pre_act * (1.0 / math.sqrt(2.0))))
    phi_small = jnp.exp(-0.5 * pre_act * pre_act) * (1.0 / math.sqrt(2.0 * math.pi))
    return pre_act * phi_big, phi_big + pre_act * phi_small


def ffn_step(total, acc_ref, out_refs):
    step = pl.program_id(0)

    @pl.when(step == 0)
    def _():
        acc_ref[...] = total

    @pl.when(step > 0)
    def _():
        acc_ref[...] += total

    @pl.when(step == pl.num_programs(0) - 1)
    def _():
        fill(out_refs, acc_ref)


def ffn_kernel(up_ref, up2_ref, dn_ref, dn2_ref, *refs, pieces):
    sources, (act_ref, slope_ref), out_refs, (acc_ref, x_ref) = refs[:pieces], refs[pieces : pieces + 2], refs[pieces + 2 : -2], refs[-2:]

    @pl.when(pl.program_id(0) == 0)
    def _():
        load(sources, x_ref)

    total = None
    for side, (up, down) in enumerate(((up_ref, dn_ref), (up2_ref, dn2_ref))):
        act, slope = gelu_pair(dot(x_ref[...], up[...], NN))
        act = act.astype(BF16)
        act_ref[side] = act
        slope_ref[side] = slope
        term = dot(act, flat(down), NN)
        total = term if total is None else total + term
    ffn_step(total, acc_ref, out_refs)


def ffn_specs(pieces, ups, downs):
    length, model = rows_of(pieces)
    hidden = ups[0].shape[1]
    step = min(256, hidden)
    cols = pl.BlockSpec((model, step), lambda i: (0, i))
    rows = pl.BlockSpec((step, model), lambda i: (i, 0))
    other_rows = rows
    if downs[1].ndim == 3:
        share = hidden // downs[1].shape[0]
        other_rows = pl.BlockSpec((step // share, share, model), lambda i: (i, 0, 0))
    made = pl.BlockSpec((2, length, step), lambda i: (0, 0, i))
    scratch = [pltpu.VMEM((length, model), F32), pltpu.VMEM((length, model), BF16)]
    return length, model, hidden, step, [cols, cols, rows, other_rows], made, [whole(piece) for piece in pieces], scratch


def ffn(pieces, ups, downs, group):
    length, model, hidden, step, specs, made, piece_specs, scratch = ffn_specs(pieces, ups, downs)
    outs, out_specs = block_outs(length, model, group)
    acts, slopes, *parts = call(
        partial(ffn_kernel, pieces=len(pieces)), "ffn",
        [((2, length, hidden), BF16), ((2, length, hidden), F32)] + outs,
        [*far(ups), *far(downs), *pieces], grid=(hidden // step,), in_specs=specs + piece_specs,
        out_specs=[made, made] + out_specs, scratch=scratch, flops=8 * length * model * hidden, exps=4 * length * hidden,
    )
    return parts, acts, slopes


def ffn_back_kernel(up_ref, up2_ref, dn_ref, dn2_ref, slope_ref, *refs, pieces):
    sources, dz_ref, out_refs, (acc_ref, g_ref) = refs[:pieces], refs[pieces], refs[pieces + 1 : -2], refs[-2:]

    @pl.when(pl.program_id(0) == 0)
    def _():
        load(sources, g_ref)

    total = None
    for side, (up, down) in enumerate(((up_ref, dn_ref), (up2_ref, dn2_ref))):
        grad_pre = (slope_ref[side] * dot(g_ref[...], flat(down), NT)).astype(BF16)
        dz_ref[side] = grad_pre
        term = dot(grad_pre, up[...], NT)
        total = term if total is None else total + term
    ffn_step(total, acc_ref, out_refs)


def ffn_back(pieces, ups, downs, slopes, group):
    length, model, hidden, step, specs, made, piece_specs, scratch = ffn_specs(pieces, ups, downs)
    outs, out_specs = block_outs(length, model, group)
    grad_pre, *parts = call(
        partial(ffn_back_kernel, pieces=len(pieces)), "ffn_back", [((2, length, hidden), BF16)] + outs,
        [*far(ups), *far(downs), far(slopes), *pieces], grid=(hidden // step,), in_specs=specs + [made] + piece_specs,
        out_specs=[made] + out_specs, scratch=scratch, flops=8 * length * model * hidden,
    )
    return parts, grad_pre


def ffn_grads_kernel(dz_ref, act_ref, *refs):
    sources, (out_ref, x_ref, g_ref) = refs[:-3], refs[-3:]

    @pl.when((pl.program_id(0) == 0) & (pl.program_id(1) == 0))
    def _():
        load(sources[: len(sources) // 2], x_ref)
        load(sources[len(sources) // 2 :], g_ref)

    out_ref[0, 0] = dot(dz_ref[0], x_ref[...], TN).astype(BF16)
    out_ref[0, 1] = dot(act_ref[0], g_ref[...], TN).astype(BF16)


def ffn_grads(pieces, grads, grad_pre, acts):
    length, model = rows_of(pieces)
    hidden = acts.shape[2]
    step = min(256, hidden)
    made = pl.BlockSpec((1, length, step), lambda s, i: (s, 0, i))
    return call(
        ffn_grads_kernel, "ffn_grads", [((2, 2, hidden, model), BF16)], [grad_pre, far(acts), *far(pieces), *grads],
        grid=(2, hidden // step), in_specs=[made, made] + [whole(p) for p in (*pieces, *grads)],
        out_specs=[pl.BlockSpec((1, 2, step, model), lambda s, i: (s, 0, i, 0))],
        scratch=[pltpu.VMEM((length, model), BF16)] * 2, flops=8 * length * model * hidden,
    )[0]


class Places:
    def __init__(self):
        self.dp_size = lax.axis_size("dp")
        self.tensor_size = lax.axis_size("tensor")
        self.group = self.tensor_size // 2
        self.dp_index = lax.axis_index("dp")
        tensor_index = lax.axis_index("tensor")
        self.core = self.dp_index % 2
        self.place = tensor_index % self.group
        self.pieces = 2 if self.group == 4 else 1

    def swap(self, value):
        pairs = []
        for dp_index in range(self.dp_size):
            for tensor_index in range(self.tensor_size):
                pair, core = divmod(dp_index, 2)
                side, place = divmod(tensor_index, self.group)
                pairs.append(
                    (
                        dp_index * self.tensor_size + tensor_index,
                        (2 * pair + side) * self.tensor_size + core * self.group + place,
                    )
                )
        return lax.ppermute(value, ("dp", "tensor"), pairs)

    def other_core(self, value):
        return lax.ppermute(value, "dp", [(d, d ^ 1) for d in range(self.dp_size)])

    def partner(self, value):
        return lax.ppermute(value, "tensor", [(t, t ^ self.group) for t in range(self.tensor_size)])

    def mate(self, value, offset):
        return lax.ppermute(value, "tensor", [(t, t ^ offset) for t in range(self.tensor_size)])

    def gather(self, pieces):
        if self.pieces == 2:
            low, high = pieces
            low_1, high_2 = self.mate(low, 1), self.mate(high, 2)
            high_1, low_2 = self.mate(high, 1), self.mate(low, 2)
            high_3, low_3 = self.mate(high_2, 1), self.mate(low_1, 2)
            return [low, high, low_1, high_1, low_2, high_2, low_3, high_3]
        return list(pieces) + [self.mate(pieces[0], o) for o in range(1, self.group)]

    def gather_beside(self, block):
        return [block] + [self.mate(block, o) for o in range(1, self.group)]

    def scatter(self, parts):
        return [parts[0]] + [self.mate(parts[o], o) for o in range(1, self.group)]

    def share(self, stacked):
        rows = stacked.shape[0] // self.dp_size
        return lax.dynamic_slice_in_dim(stacked, self.dp_index * rows, rows, 0)

    def split(self, weights):
        rows = weights.shape[1] // self.dp_size
        return lax.dynamic_slice_in_dim(weights, self.dp_index * rows, rows, 1)

    def whole(self, share):
        return lax.all_gather(share, "dp", axis=0)

    def whole_rows(self, share):
        return lax.all_gather(share, "dp", axis=0, tiled=True)

    def sum_weights(self, grads):
        shape = grads.shape
        summed = lax.psum_scatter(grads.reshape(-1, shape[-1]), "dp", scatter_dimension=1, tiled=True)
        return summed.reshape(*shape[:-1], -1)

    def sum_weights_now(self, grads):
        if self.dp_size != 4:
            return self.sum_weights(grads)
        width = grads.shape[-1] // 4
        blocks = [grads[..., i * width : (i + 1) * width] for i in range(4)]
        first = self.core == 0

        def pick(if_first, low, high):
            return jnp.where(if_first, low, high)

        kept = jnp.concatenate([pick(first, *blocks[:2]), pick(first, *blocks[2:])], axis=-1)
        sent = jnp.concatenate([pick(first, *blocks[1::-1]), pick(first, *blocks[:1:-1])], axis=-1)
        kept = kept.astype(F32) + self.other_core(sent).astype(F32)
        low, high = kept[..., :width], kept[..., width:]
        first = self.dp_index < 2
        sent = pick(first, high, low).astype(BF16)
        received = lax.ppermute(sent, "dp", [(d, d ^ 2) for d in range(4)])
        return (pick(first, low, high) + received.astype(F32)).astype(BF16)

    def marks(self, seg_row, seg_key_row):
        kinds = jnp.arange(SEGMENTS)[:, None] - 1
        length = seg_row.shape[0] // self.tensor_size
        order = self.place ^ jnp.arange(self.group)
        blocks = jnp.concatenate([self.core * self.group + order, (1 - self.core) * self.group + order])
        own = jnp.take(seg_row.reshape(-1, length), blocks[: self.group], axis=0).reshape(1, -1)
        keys = jnp.take(seg_key_row.reshape(-1, length), blocks, axis=0).reshape(1, -1)
        positions = (blocks[: self.group, None] * length + jnp.arange(length)[None, :]).reshape(1, -1)
        return (
            ((own == kinds) | (own < 0)).astype(BF16),
            (keys == kinds).astype(BF16),
            positions,
            jnp.broadcast_to(blocks[:, None] * length, (blocks.shape[0], own.shape[1])),
        )


def route(places, token_ids, token_live, shard_rows):
    owners = places.dp_size * places.tensor_size
    tokens = token_ids.shape[0]
    capacity = max(2, 3 * tokens // (2 * owners))
    owner = token_ids // shard_rows
    row = token_ids - owner * shard_rows
    earlier = jnp.arange(tokens)[None, :] < jnp.arange(tokens)[:, None]
    same = (owner[:, None] == owner[None, :]) & token_live[None, :] & earlier
    ranking = jnp.sum(same.astype(jnp.int32), axis=1)
    slot = jnp.where(token_live, owner * capacity + ranking, -1)
    picks = jnp.arange(owners * capacity)[:, None] == slot[None, :]
    requests = jnp.sum(jnp.where(picks, row[None, :] + 1, 0), axis=1) - 1
    return picks.astype(BF16), requests.reshape(owners, capacity)


LANES = 128


def to_owners(places, rows, capacity):
    owners = places.dp_size * places.tensor_size
    runs = rows.reshape(owners, capacity * rows.shape[1] // LANES, LANES)
    moved = lax.all_to_all(runs, ("dp", "tensor"), split_axis=0, concat_axis=0, tiled=True)
    return moved.reshape(rows.shape)


def finish_kernel(*refs, count):
    parts, outs = refs[: 2 * count], refs[2 * count :]
    for i in range(count):
        own_ref, other_ref = parts[2 * i], parts[2 * i + 1]
        in_ref, out_ref = outs[2 * i], outs[2 * i + 1]
        for j in range(3):
            in_ref[j] = (own_ref[j].astype(F32) + other_ref[j].astype(F32)).T
        out_ref[...] = own_ref[3].astype(F32) + other_ref[3].astype(F32)


def finish_attention(*pairs):
    _, shard, width = pairs[0][0].shape
    return call(
        partial(finish_kernel, count=len(pairs)), "finish",
        [((3, width, shard), F32), ((shard, width), F32)] * len(pairs), [part for pair in pairs for part in pair],
    )


def finish_kernel(*refs, count):
    parts, outs = refs[: 2 * count], refs[2 * count :]
    for i in range(count):
        own_ref, other_ref = parts[2 * i], parts[2 * i + 1]
        in_ref, out_ref = outs[2 * i], outs[2 * i + 1]
        for j in range(3):
            in_ref[j] = (own_ref[j].astype(F32) + other_ref[j].astype(F32)).T
        out_ref[...] = own_ref[3].astype(F32) + other_ref[3].astype(F32)


def finish_attention(*pairs):
    _, shard, width = pairs[0][0].shape
    return call(
        partial(finish_kernel, count=len(pairs)), "finish",
        [((3, width, shard), F32), ((shard, width), F32)] * len(pairs), [part for pair in pairs for part in pair],
    )


def send_back_kernel(picks_ref, e_ref, e2_ref, last_ref, *refs):
    gain_refs, out_ref, rows_ref = refs[:-2], refs[-2], refs[-1]
    length = e_ref.shape[0]
    rows_ref[...] = jnp.zeros_like(rows_ref)
    for i, ref in enumerate(gain_refs):
        rows_ref[i : i + 1] = ref[...]
    sent = dot(picks_ref[:, :length], e_ref[...], NN) + dot(picks_ref[:, length:], e2_ref[...], NN)
    out_ref[...] = (sent + dot(last_ref[...], rows_ref[...].astype(BF16), NN)).astype(BF16)


def send_back(picks, src_grad, tgt_grad, gains, capacity):
    owners = picks.shape[0] // capacity
    slots = jnp.arange(owners * (capacity + 1))
    owner, slot = slots // (capacity + 1), slots % (capacity + 1)
    wider = jnp.take(picks, jnp.minimum(owner * capacity + slot, picks.shape[0] - 1), axis=0)
    wider = jnp.where((slot < capacity)[:, None], wider, jnp.zeros_like(wider))
    rows = 16
    last = (slot == capacity)[:, None] & (owner[:, None] == jnp.arange(rows)[None, :])
    return call(
        send_back_kernel, "send_back", [((slots.shape[0], src_grad.shape[1]), BF16)],
        [wider, src_grad, tgt_grad, last.astype(BF16), *gains], scratch=[pltpu.VMEM((rows, src_grad.shape[1]), F32)],
        flops=2 * wider.size * src_grad.shape[1],
    )[0]


def on_device(
    src_ids,
    tgt_ids,
    src_segs,
    tgt_segs,
    embed_table,
    norm_gains,
    enc_qkv,
    enc_out,
    enc_up,
    enc_down,
    dec_qkv,
    dec_out,
    cross_q,
    cross_kv,
    cross_out,
    dec_up,
    dec_down,
    cotangent,
):
    places = Places()
    group = places.group
    local_len = src_ids.shape[0]
    shard_rows, model = embed_table.shape
    root = math.sqrt(model)
    shard = enc_qkv.shape[2]
    count = places.pieces

    tensor_at = lax.axis_index("tensor") * local_len
    rows_here = [src_segs.reshape(-1), tgt_segs.reshape(-1)]
    ids_here = jnp.concatenate([src_ids.reshape(-1), tgt_ids.reshape(-1)])
    live_here = jnp.concatenate([lax.dynamic_slice_in_dim(row, tensor_at, local_len, 0) for row in rows_here]) >= 0
    enc_in_share = places.partner(places.split(enc_qkv))
    requests = route(places, ids_here, live_here, shard_rows)[1]
    capacity = requests.shape[1]
    moved = places.swap(jnp.concatenate([ids_here] + rows_here))
    wanted = lax.all_to_all(requests, ("dp", "tensor"), split_axis=0, concat_axis=0, tiled=True)
    wanted = wanted.reshape(-1, 2, 2, group * capacity).swapaxes(1, 2).reshape(-1)
    wanted = after(wanted, moved, enc_in_share)
    found = wanted >= 0
    picked = jnp.take(embed_table, jnp.maximum(wanted, 0), axis=0, mode="clip")
    replies = to_owners(places, picked, capacity)
    outs_share = jnp.concatenate([places.share(weight) for weight in (enc_out, dec_out, cross_out)])
    outs_share = places.partner(after(outs_share, picked))
    replies = after(replies, outs_share)
    cross_share = jnp.concatenate([places.split(cross_q[None]), places.split(cross_kv)])

    token_ids = moved[: 2 * local_len]
    src_row, tgt_row = jnp.split(moved[2 * local_len :], 2)
    offset = (places.core * group + places.place) * local_len
    live = [lax.dynamic_slice_in_dim(row, offset, local_len, 0) >= 0 for row in (src_row, tgt_row)]
    picks = route(places, token_ids, jnp.concatenate(live), shard_rows)[0]
    enc_marks = places.marks(src_row, src_row)
    dec_marks = places.marks(tgt_row, tgt_row)
    cross_marks = places.marks(tgt_row, src_row)

    def narrow(own, own_index, other, other_index):
        if own.ndim == 2:
            own_part = (own, own.shape, (0, 0))
        else:
            own_part = (own, (1, *own.shape[1:]), (own_index, 0, 0))
        return own_part, (other, (other.shape[0], 1, *other.shape[2:]), (0, other_index, 0, 0))

    def wide(own, other, index):
        rows = own.shape[0] // places.dp_size
        return (own, own.shape, (0, 0)), (other, (other.shape[0], rows, model), (0, index, 0))

    def narrow_whole(share, start):
        share = after(share, start)
        return places.whole(jnp.concatenate([share, share]))

    enc_in_other = narrow_whole(enc_in_share, picked)
    enc_in = [narrow(enc_qkv, i, enc_in_other, i) for i in range(3)]

    token_shape = (local_len, model)
    embeds, h0, t0, *pieces = call(
        partial(embed_kernel, root=root), "embed",
        [((2 * local_len, model), BF16), (token_shape, F32), (token_shape, F32)] + [((local_len // count, model), BF16)] * count + [(token_shape, BF16)],
        [picks, replies, norm_gains],
    )
    a1, c1 = pieces[:-1], pieces[-1]
    down_rows = enc_down.shape[0] // places.dp_size
    out_rows = shard // places.dp_size
    outs_other = narrow_whole(outs_share, a1)
    dec_in_share = places.partner(after(places.split(dec_qkv), a1))
    a1 = places.gather(a1)
    c1 = places.gather_beside(after(c1, a1))
    out_rows = shard // places.dp_size
    if out_rows % 8:
        outs_other = [outs_other[:, i * out_rows : (i + 1) * out_rows] for i in range(3)]
        enc_o, dec_o, cross_o = [wide(own, other, 0) for own, other in zip((enc_out, dec_out, cross_out), outs_other)]
    else:
        enc_o, dec_o, cross_o = [wide(own, outs_other, i) for i, own in enumerate((enc_out, dec_out, cross_out))]
    enc_q, enc_mine = project(a1, enc_in, shard, True)
    dec_in_other = narrow_whole(dec_in_share, enc_mine)
    dec_in = [narrow(dec_qkv, i, dec_in_other, i) for i in range(3)]
    enc_theirs = places.other_core(enc_mine)
    parts, enc_mixed, enc_stats = attend(enc_q, enc_mine, enc_theirs, enc_o, enc_marks, False, model, group)
    enc_up_share = places.partner(after(places.share(enc_up), enc_mine))
    enc_down_share = places.partner(after(places.share(enc_down), enc_mine))
    own_parts = after(parts, enc_up_share, c1)
    enc_ups = [enc_up, places.whole_rows(after(enc_up_share, own_parts))]
    parts = places.scatter(own_parts)
    dec_q, dec_mine = project(after(c1, own_parts), dec_in, shard, True)
    dec_theirs = places.other_core(dec_mine)
    cross_share = places.partner(after(cross_share, dec_mine))
    cot_moved = places.swap(after(cotangent.reshape(token_shape).astype(BF16), dec_mine))
    dec_parts, dec_mixed, dec_stats = attend(
        after(dec_q, enc_down_share), dec_mine, dec_theirs, dec_o, dec_marks, True, model, group
    )
    enc_downs = [enc_down, places.whole_rows(after(enc_down_share, dec_q))]
    h1, own_b1 = sum_norm(h0, after(parts, dec_parts, cot_moved), norm_gains, 2, count)

    b1 = places.gather(own_b1)
    cross_other = narrow_whole(cross_share, own_b1)
    dec_parts = places.scatter(after(dec_parts, own_b1))
    t1, (own_c2,) = sum_norm(t0, after(dec_parts, b1), norm_gains, 6, 1)
    dec_up_share = places.partner(after(places.share(dec_up), own_c2))
    b1 = after(b1, own_c2)
    c2 = places.gather_beside(own_c2)
    own_parts, enc_acts, enc_slopes = ffn(b1, enc_ups, enc_downs, group)
    own_parts = after(own_parts, c2)
    cross_in = narrow(cross_q, 0, cross_other, 0)
    cross_mem = [narrow(cross_kv, i, cross_other, 1 + i) for i in range(2)]
    parts = places.scatter(own_parts)
    h2, own_memory = sum_norm(h1, parts, norm_gains, 3, count)
    dec_ups = [dec_up, places.whole_rows(after(dec_up_share, own_memory))]
    memory = places.gather(own_memory)
    cross_qs = project(after(c2, own_memory), [cross_in], shard, True)[0]
    cross_mine = project(after(memory, cross_qs), cross_mem, shard, False)[0]
    dec_down_share = places.partner(after(places.share(dec_down), cross_mine))
    cross_theirs = places.other_core(cross_mine)
    parts, cross_mixed, cross_stats = attend(
        cross_qs, cross_mine, cross_theirs, cross_o, cross_marks, False, model, group
    )
    dec_downs = [dec_down, places.whole_rows(after(dec_down_share, parts))]
    t2, own_f1 = sum_norm(t1, places.scatter(parts), norm_gains, 7, count)
    f1 = places.gather(own_f1)
    parts, dec_acts, dec_slopes = ffn(f1, dec_ups, dec_downs, group)
    decoded, grad_t, pieces, gain_final = final(
        t2, places.scatter(parts), norm_gains, live[1][:, None].astype(F32), cot_moved, 8, count
    )

    grad_full = places.gather(pieces)
    decoded = places.swap(after(decoded, grad_full))
    own_parts, grad_pre = ffn_back(grad_full, dec_ups, dec_downs, dec_slopes, group)
    dec_ffn_grads = ffn_grads(f1, after(grad_full, own_parts), grad_pre, dec_acts)
    parts = after(places.scatter(own_parts), dec_ffn_grads)
    grad_t, pieces, gain_dffn = norm_back(grad_t, parts, t2, norm_gains, 7, count)

    dec_ffn_sum = places.sum_weights(after(dec_ffn_grads, pieces))
    grad_full = after(places.gather(pieces), decoded)
    grad_q, mine, theirs = attend_back(
        grad_full, cross_o, cross_qs, cross_mine, cross_theirs, cross_marks, cross_stats, False
    )
    theirs = places.other_core(theirs)
    own_parts = unproject(grad_q, cross_in, model, group)
    own_mem_parts, grad_kv = unproject_keys(None, mine, after(theirs, own_parts), cross_mem, model, group)
    mem_parts = places.scatter(own_mem_parts)
    cross_grads = attend_grads(grad_q, grad_kv, cross_mixed, far(c2), after(grad_full, own_mem_parts), far(memory))
    grad_h, pieces_h, gain_memory = norm_back(None, after(mem_parts, cross_grads), h2, norm_gains, 3, count)
    cross_sum = places.sum_weights(after(cross_grads, pieces_h))

    def finish(summed, other):
        return summed[0].astype(F32) + other.astype(F32)

    def turned(grads):
        return jnp.swapaxes(grads, -1, -2)

    enc_full = places.gather(pieces_h)
    parts = places.scatter(after(own_parts, enc_full))
    dec_ffn_other = places.partner(after(dec_ffn_sum[1], enc_full))
    own_parts, grad_pre = ffn_back(enc_full, enc_ups, enc_downs, enc_slopes, group)
    h_parts = places.scatter(own_parts)
    enc_ffn_grads = ffn_grads(b1, after(enc_full, own_parts), grad_pre, enc_acts)
    grad_t, pieces, gain_cross = norm_back(grad_t, after(parts, enc_ffn_grads, dec_ffn_sum), t1, norm_gains, 6, count)
    dec_full = places.gather(pieces)
    grad_h, pieces_h, gain_effn = norm_back(grad_h, after(h_parts, pieces), h1, norm_gains, 2, 1)
    hidden_full = places.gather_beside(pieces_h[0])
    dec_full = after(dec_full, pieces_h, dec_ffn_other)
    cross_sum_other = places.partner(after(cross_sum[1], dec_full))
    enc_ffn_sum = places.sum_weights(after(enc_ffn_grads, cross_sum, pieces_h))
    grad_q, mine, theirs = attend_back(dec_full, dec_o, dec_q, dec_mine, dec_theirs, dec_marks, dec_stats, True)
    theirs = places.other_core(theirs)
    own_parts, grad_kv = unproject_keys(grad_q, mine, theirs, dec_in, model, group)
    dec_parts = places.scatter(own_parts)
    dec_grads = attend_grads(grad_q, grad_kv, dec_mixed, far(c1), after(dec_full, own_parts))

    grad_full = after(hidden_full, dec_grads, cross_sum_other)
    grad_q, mine, theirs = attend_back(grad_full, enc_o, enc_q, enc_mine, enc_theirs, enc_marks, enc_stats, False)
    theirs = places.other_core(theirs)
    dec_sum = places.sum_weights(after(dec_grads, enc_ffn_sum, grad_full))
    own_parts, grad_kv = unproject_keys(grad_q, mine, theirs, enc_in, model, group)
    parts = places.scatter(own_parts)
    dec_ffn_sum = finish(dec_ffn_sum, dec_ffn_other)
    dec_ffn_outs = turned(dec_ffn_sum[0]), dec_ffn_sum[1]
    cross_sum = finish(cross_sum, cross_sum_other)
    cross_outs = turned(cross_sum[0]), turned(cross_sum[1:3]), cross_sum[3]
    decoded_out = decoded.astype(F32)[:, None]
    dec_ffn_outs, cross_outs, decoded_out = lax.optimization_barrier((dec_ffn_outs, cross_outs, decoded_out))
    tgt_grad, gain_dattn, gain_demb = embed_back(
        grad_t, after(dec_parts, own_parts, dec_ffn_outs, cross_outs, decoded_out), t0, embeds[local_len:], norm_gains, 4, root
    )
    src_grad, gain_eattn, gain_eemb = embed_back(
        grad_h, after(parts, tgt_grad), h0, embeds[:local_len], norm_gains, 0, root
    )

    gains = [
        gain_eemb, gain_eattn, gain_effn, gain_memory, gain_demb, gain_dattn, gain_cross, gain_dffn, gain_final
    ]
    outgoing = send_back(picks, src_grad, tgt_grad, gains, capacity)
    arrived = to_owners(places, outgoing, capacity + 1).reshape(-1, capacity + 1, model)
    enc_grads = attend_grads(grad_q, grad_kv, enc_mixed, far(a1), after(grad_full, outgoing))
    enc_sum = places.sum_weights_now(enc_grads)
    enc_ffn_other = places.partner(after(enc_ffn_sum[1], outgoing))
    arrived = after(arrived, enc_sum, enc_ffn_other)
    last_other = places.partner(after(jnp.stack([dec_sum[1], enc_sum[1]]), arrived))
    gain_sum = jnp.sum(arrived[:, capacity].astype(F32), axis=0)
    gain_grad = lax.all_to_all(
        jnp.broadcast_to(gain_sum[None], (arrived.shape[0], model)), ("dp", "tensor"), 0, 0, tiled=True
    )[: len(gains)]
    counts = jnp.sum(((wanted[:, None] == wanted[None, :]) & found[None, :]).astype(F32), axis=1)
    rows = arrived[:, :capacity].reshape(-1, model).astype(F32) / jnp.maximum(counts, 1.0)[:, None]
    target_rows = jnp.where(found, wanted, shard_rows)
    table_grad = jnp.zeros((shard_rows, model), F32).at[target_rows].add(rows, mode="drop")

    enc_ffn_sum = finish(enc_ffn_sum, enc_ffn_other)
    dec_in_grad, dec_out_grad, enc_in_grad, enc_out_grad = finish_attention(
        (dec_sum[0], last_other[0]), (enc_sum[0], last_other[1])
    )

    return (
        decoded_out,
        table_grad,
        gain_grad,
        enc_in_grad,
        enc_out_grad,
        turned(enc_ffn_sum[0]),
        enc_ffn_sum[1],
        dec_in_grad,
        dec_out_grad,
        *cross_outs,
        *dec_ffn_outs,
    )


def solution(mesh):
    return jax.shard_map(
        on_device,
        mesh=mesh,
        in_specs=(
            P("tensor", "dp"),
            P("tensor", "dp"),
            P(None, "dp"),
            P(None, "dp"),
            P(("dp", "tensor"), None),
            P(),
            P(None, None, "tensor"),
            P("tensor", None),
            P(None, "tensor"),
            P("tensor", None),
            P(None, None, "tensor"),
            P("tensor", None),
            P(None, "tensor"),
            P(None, None, "tensor"),
            P("tensor", None),
            P(None, "tensor"),
            P("tensor", None),
            P("tensor", "dp", None),
        ),
        out_specs=(
            P("tensor", "dp", None),
            P(("dp", "tensor"), None),
            P(),
            P(None, "dp", "tensor"),
            P("tensor", "dp"),
            P("dp", "tensor"),
            P("tensor", "dp"),
            P(None, "dp", "tensor"),
            P("tensor", "dp"),
            P("dp", "tensor"),
            P(None, "dp", "tensor"),
            P("tensor", "dp"),
            P("dp", "tensor"),
            P("tensor", "dp"),
        ),
        check_vma=False,
    )
```

```python
import math
from functools import partial

import jax
import jax.numpy as jnp
from jax import lax
from jax.experimental import pallas as pl
from jax.experimental.pallas import tpu as pltpu
from jax.sharding import PartitionSpec as P

HEAD_DIM = 64
FACTOR = 0.125

NORM_EPS = 1e-05
MASKED = -1e30
SEGMENTS = 8
F32 = jnp.float32
BF16 = jnp.bfloat16
VMEM_LIMIT = 48 << 20

NN = ((1,), (0,))
NT = ((1,), (1,))
TN = ((0,), (0,))


def dot(lhs, rhs, dims):
    return lax.dot_general(lhs, rhs, (dims, ((), ())), preferred_element_type=F32)


def call(kernel, name, outs, args, grid=(), in_specs=None, out_specs=None, scratch=(), flops=0, exps=0):
    out_shape = [jax.ShapeDtypeStruct(shape, dtype) for shape, dtype in outs]
    moved = sum(math.prod(a.shape) * a.dtype.itemsize for a in list(args) + out_shape)
    specs = {}
    if in_specs is not None:
        specs = dict(in_specs=in_specs, out_specs=out_specs)
    return pl.pallas_call(
        kernel,
        grid=grid,
        out_shape=out_shape,
        scratch_shapes=list(scratch),
        compiler_params=pltpu.CompilerParams(vmem_limit_bytes=VMEM_LIMIT),
        cost_estimate=pl.CostEstimate(flops=flops // 50, transcendentals=exps // 50, bytes_accessed=moved // 50),
        name=name,
        **specs,
    )(*args)


def normal_form(values):
    shifted = values - jnp.mean(values, axis=-1, keepdims=True)
    scale = lax.rsqrt(jnp.mean(shifted * shifted, axis=-1, keepdims=True) + NORM_EPS)
    return shifted * scale, scale


def norm_grad(values, gain, grad):
    normed, scale = normal_form(values)
    inner = grad * gain
    drop = jnp.mean(inner, axis=-1, keepdims=True) + normed * jnp.mean(inner * normed, axis=-1, keepdims=True)
    return scale * (inner - drop), jnp.sum(grad * normed, axis=0, keepdims=True)


def sum_parts(refs):
    total = refs[0][...].astype(F32)
    for ref in refs[1:]:
        total = total + ref[...].astype(F32)
    return total


def fill(refs, value):
    at = 0
    for ref in refs:
        ref[...] = value[at : at + ref.shape[0]].astype(ref.dtype)
        at += ref.shape[0]


def load(refs, scratch):
    at = 0
    for ref in refs:
        scratch[at : at + ref.shape[0]] = ref[...]
        at += ref.shape[0]


def piece_outs(state, count):
    return [((state.shape[0] // count, state.shape[1]), BF16)] * count


def embed_kernel(picks_ref, replies_ref, gains_ref, e_ref, h_ref, t_ref, *out_refs, root):
    length = h_ref.shape[0]
    rows = dot(picks_ref[...], replies_ref[...], TN)
    e_ref[...] = rows.astype(BF16)
    for start, first, state_ref, outs in ((0, 0, h_ref, out_refs[:-1]), (length, 4, t_ref, out_refs[-1:])):
        state = normal_form(rows[start : start + length] * root)[0] * gains_ref[first : first + 1, :]
        state_ref[...] = state
        fill(outs, normal_form(state)[0] * gains_ref[first + 1 : first + 2, :])


def sum_norm_kernel(state_ref, gains_ref, *refs, index, group):
    state = state_ref[...] + sum_parts(refs[:group])
    refs[group][...] = state
    fill(refs[group + 1 :], normal_form(state)[0] * gains_ref[index : index + 1, :])


def sum_norm(state, parts, gains, index, count):
    new, *pieces = call(
        partial(sum_norm_kernel, index=index, group=len(parts)), "sum_norm",
        [(state.shape, F32)] + piece_outs(state, count), [state, gains, *parts], flops=12 * state.size,
    )
    return new, pieces


def final_kernel(state_ref, gains_ref, live_ref, cot_ref, *refs, index, group):
    state = state_ref[...] + sum_parts(refs[:group])
    dec_ref, grad_ref, dg_ref, *outs = refs[group:]
    gain = gains_ref[index : index + 1, :]
    live = live_ref[...]
    dec_ref[...] = (normal_form(state)[0] * gain * live).astype(BF16)
    grad, dg_ref[...] = norm_grad(state, gain, cot_ref[...].astype(F32) * live)
    grad_ref[...] = grad
    fill(outs, grad)


def final(state, parts, gains, live, cotangent, index, count):
    decoded, grad, gain_grad, *pieces = call(
        partial(final_kernel, index=index, group=len(parts)), "final",
        [(state.shape, BF16), (state.shape, F32), ((1, state.shape[1]), F32)] + piece_outs(state, count),
        [state, gains, live, cotangent, *parts], flops=40 * state.size,
    )
    return decoded, grad, pieces, gain_grad


def norm_back_kernel(state_ref, gains_ref, *refs, index, group, adds):
    grad, dg = norm_grad(state_ref[...], gains_ref[index : index + 1, :], sum_parts(refs[:group]))
    refs = refs[group:]
    if adds:
        grad = grad + refs[0][...]
        refs = refs[1:]
    refs[0][...] = grad
    refs[1][...] = dg
    fill(refs[2:], grad)


def norm_back(grad, parts, state, gains, index, count):
    new, gain_grad, *pieces = call(
        partial(norm_back_kernel, index=index, group=len(parts), adds=grad is not None), "norm_back",
        [(state.shape, F32), ((1, state.shape[1]), F32)] + piece_outs(state, count),
        [far(state), gains, *parts] + ([] if grad is None else [grad]), flops=20 * state.size,
    )
    return new, pieces, gain_grad


def embed_back_kernel(grad_ref, state_ref, rows_ref, gains_ref, *refs, index, root, group):
    e_ref, dg_ref, de_ref = refs[group:]
    grad, dg_ref[...] = norm_grad(state_ref[...], gains_ref[index + 1 : index + 2, :], sum_parts(refs[:group]))
    rows = rows_ref[...].astype(F32) * root
    grad, de_ref[...] = norm_grad(rows, gains_ref[index : index + 1, :], grad + grad_ref[...])
    e_ref[...] = (grad * root).astype(BF16)


def embed_back(grad, parts, state, rows, gains, index, root):
    width = state.shape[1]
    return call(
        partial(embed_back_kernel, index=index, root=root, group=len(parts)), "embed_back",
        [(state.shape, BF16), ((1, width), F32), ((1, width), F32)], [grad, far(state), far(rows), gains, *parts],
        flops=40 * state.size,
    )


def weight_specs(weights):
    operands, specs = [], []
    for weight in weights:
        for array, block, index in weight:
            operands.append(far(array))
            specs.append(pl.BlockSpec(block, lambda *_, index=index: index))
    return operands, specs


def flat(ref):
    return ref[...].reshape(-1, ref.shape[-1])


def after(value, *others):
    return lax.optimization_barrier((value, *others))[0]


def far(values):
    return jax.tree.map(lambda value: pltpu.with_memory_space_constraint(value, pltpu.HBM), values)


def whole(array):
    return pl.BlockSpec(array.shape, lambda *_, rank=len(array.shape): (0,) * rank)


def pair_cols(own_ref, other_ref):
    return jnp.concatenate([flat(own_ref), flat(other_ref)], axis=1)


def project_kernel(*refs, pieces, count, scaled):
    x_ref = refs[-1]
    load(refs[:pieces], x_ref)
    refs = refs[pieces:-1]
    values = x_ref[...]
    for i in range(count):
        made = dot(values, pair_cols(refs[2 * i], refs[2 * i + 1]), NN).astype(BF16)
        if scaled and i == 0:
            refs[2 * count][...] = made * jnp.asarray(FACTOR, BF16)
        else:
            out_ref = refs[-1]
            at = (i - int(scaled)) * made.shape[1]
            out_ref[:, at : at + made.shape[1]] = made


def rows_of(pieces):
    return sum(piece.shape[0] for piece in pieces), pieces[0].shape[1]


def project(pieces, weights, shard, scaled):
    length, width = rows_of(pieces)
    operands, specs = weight_specs(weights)
    others = len(weights) - int(scaled)
    outs = [((length, 2 * shard), BF16)] * int(scaled) + [((length, 2 * shard * others), BF16)] * int(others > 0)
    return call(
        partial(project_kernel, pieces=len(pieces), count=len(weights), scaled=scaled), "project", outs,
        [*pieces, *operands], grid=(1,), in_specs=[whole(piece) for piece in pieces] + specs,
        out_specs=[pl.BlockSpec(shape, lambda *_: (0, 0)) for shape, _ in outs],
        scratch=[pltpu.VMEM((length, width), BF16)], flops=4 * length * width * shard * len(weights),
    )


def block_outs(length, width, group):
    shape = (length // group, width)
    return [(shape, BF16)] * group, [pl.BlockSpec(shape, lambda *_: (0, 0))] * group


def unproject_kernel(x_ref, own_ref, other_ref, *out_refs):
    fill(out_refs, dot(x_ref[...], pair_cols(own_ref, other_ref), NT))


def unproject(values, weight, width, group):
    operands, specs = weight_specs([weight])
    outs, out_specs = block_outs(values.shape[0], width, group)
    return call(
        unproject_kernel, "unproject", outs, [values] + operands, grid=(1,), in_specs=[whole(values)] + specs,
        out_specs=out_specs, flops=2 * values.size * width,
    )


def unproject_keys_kernel(*refs, lead, group):
    if lead:
        dq_ref, refs = refs[0], refs[1:]
    mine_ref, theirs_ref = refs[0], refs[1]
    weights, sum_ref, out_refs = refs[2 : -group - 1], refs[-group - 1], refs[-group:]
    summed = (mine_ref[...] + theirs_ref[...].astype(F32)).astype(BF16)
    sum_ref[...] = summed
    span = summed.shape[1] // 2
    total = dot(summed[:, :span], pair_cols(*weights[-4:-2]), NT) + dot(summed[:, span:], pair_cols(*weights[-2:]), NT)
    if lead:
        total = total + dot(dq_ref[...], pair_cols(*weights[:2]), NT)
    fill(out_refs, total)


def unproject_keys(queries_grad, mine, theirs, weights, width, group):
    lead = queries_grad is not None
    operands, specs = weight_specs(weights)
    values = ([queries_grad] if lead else []) + [mine, theirs]
    outs, out_specs = block_outs(mine.shape[0], width, group)
    summed, *parts = call(
        partial(unproject_keys_kernel, lead=lead, group=group), "unproject_keys", [(theirs.shape, BF16)] + outs,
        values + operands, grid=(1,), in_specs=[whole(v) for v in values] + specs, out_specs=[whole(theirs)] + out_specs,
        flops=2 * mine.size * width * len(weights) // 2,
    )
    return parts, summed


def mask_block(sq_ref, sk_ref, pq_ref, base_ref, causal):
    seen = dot(sk_ref[...], sq_ref[...], TN)
    if causal:
        blocks = base_ref.shape[0]
        size = seen.shape[0] // blocks
        index = lax.broadcasted_iota(jnp.int32, (size, seen.shape[1]), 0)
        passed = pq_ref[...]
        seen = jnp.concatenate(
            [
                jnp.where(passed >= index + base_ref[b : b + 1, :], seen[b * size : (b + 1) * size], 0.0)
                for b in range(blocks)
            ]
        )
    return (1.0 - seen) * MASKED


def gather_keys(kv_ref, mine_ref, theirs_ref):
    half = mine_ref.shape[0]
    kv_ref[:half] = mine_ref[...]
    kv_ref[half:] = theirs_ref[...]


def attend_kernel(
    q_ref, mine_ref, theirs_ref, wo_ref, wo2_ref, sq_ref, sk_ref, pq_ref, pk_ref, o_ref, st_ref, *refs, causal, heads
):
    part_refs, kv_ref, part_ref = refs[:-2], refs[-2], refs[-1]

    @pl.when(pl.program_id(0) == 0)
    def _():
        gather_keys(kv_ref, mine_ref, theirs_ref)

    width = heads * HEAD_DIM
    hidden = mask_block(sq_ref, sk_ref, pq_ref, pk_ref, causal)
    for head in range(heads):
        lo, hi = head * HEAD_DIM, (head + 1) * HEAD_DIM
        scores = dot(kv_ref[:, lo:hi], q_ref[:, lo:hi], NT) + hidden
        peak = jnp.max(scores, axis=0, keepdims=True)
        raised = jnp.exp(scores - peak)
        summed = jnp.sum(raised, axis=0, keepdims=True)
        mixed = dot(kv_ref[:, width + lo : width + hi], raised.astype(BF16), TN) * (1.0 / summed)
        o_ref[:, lo:hi] = mixed.T.astype(BF16)
        st_ref[head : head + 1, :] = peak + jnp.log(summed)
    half = width // 2
    part = dot(o_ref[:, :half], flat(wo_ref), NN) + dot(o_ref[:, half:], flat(wo2_ref), NN)
    step = part.shape[0]
    part_ref[pl.ds(pl.program_id(0) * step, step)] = part.astype(BF16)

    @pl.when(pl.program_id(0) == pl.num_programs(0) - 1)
    def _():
        fill(part_refs, part_ref)


def mask_specs(step, keys_len, blocks):
    return [
        pl.BlockSpec((SEGMENTS, step), lambda i: (0, i)),
        pl.BlockSpec((SEGMENTS, keys_len), lambda i: (0, 0)),
        pl.BlockSpec((1, step), lambda i: (0, i)),
        pl.BlockSpec((blocks, step), lambda i: (0, 0)),
    ]


def attend(queries, mine, theirs, out_weight, marks, causal, model, group):
    length, width = queries.shape
    keys_len = 2 * length
    heads = width // HEAD_DIM
    step = min(256, length)
    rows = pl.BlockSpec((step, width), lambda i: (i, 0))
    operands, specs = weight_specs([out_weight])
    outs, out_specs = block_outs(length, model, group)
    mixed, stats, *parts = call(
        partial(attend_kernel, causal=causal, heads=heads), "attend",
        [((length, width), BF16), ((heads, length), F32)] + outs,
        [queries, mine, theirs] + operands + list(marks), grid=(length // step,),
        in_specs=[rows, whole(mine), whole(theirs)] + specs + mask_specs(step, keys_len, marks[3].shape[0]),
        out_specs=[rows, pl.BlockSpec((heads, step), lambda i: (0, i))] + out_specs,
        scratch=[pltpu.VMEM((keys_len, 2 * width), BF16), pltpu.VMEM((length, model), BF16)],
        flops=4 * length * keys_len * width, exps=length * keys_len * heads,
    )
    return parts, mixed, stats


def attend_back_kernel(
    wo_ref, wo2_ref, q_ref, mine_ref, theirs_ref, sq_ref, sk_ref, pq_ref, pk_ref, st_ref, *refs, causal, heads
):
    pieces, (dq_ref, dmine_ref, dtheirs_ref, kv_ref, dkv_ref, do_ref, g_ref) = refs[:-7], refs[-7:]
    width = heads * HEAD_DIM
    half = width // 2
    step = dq_ref.shape[0]

    @pl.when(pl.program_id(0) == 0)
    def _():
        gather_keys(kv_ref, mine_ref, theirs_ref)
        dkv_ref[...] = jnp.zeros_like(dkv_ref)
        load(pieces, g_ref)

    grad = g_ref[pl.ds(pl.program_id(0) * step, step)]
    do_ref[:, :half] = dot(grad, flat(wo_ref), NT).astype(BF16)
    do_ref[:, half:] = dot(grad, flat(wo2_ref), NT).astype(BF16)
    hidden = mask_block(sq_ref, sk_ref, pq_ref, pk_ref, causal)
    for head in range(heads):
        lo, hi = head * HEAD_DIM, (head + 1) * HEAD_DIM
        queries, grads = q_ref[:, lo:hi], do_ref[:, lo:hi]
        keys, values = kv_ref[:, lo:hi], kv_ref[:, width + lo : width + hi]
        scores = dot(keys, queries, NT) + hidden
        probs = jnp.exp(scores - st_ref[head : head + 1, :])
        grad_probs = dot(values, grads, NT)
        inner = jnp.sum(probs * grad_probs, axis=0, keepdims=True)
        grad_scores = (probs * (grad_probs - inner)).astype(BF16)
        dq_ref[:, lo:hi] = (dot(keys, grad_scores, TN) * FACTOR).T.astype(BF16)
        dkv_ref[:, lo:hi] += dot(grad_scores, queries, NN)
        dkv_ref[:, width + lo : width + hi] += dot(probs.astype(BF16), grads, NN)

    @pl.when(pl.program_id(0) == pl.num_programs(0) - 1)
    def _():
        keys_half = dmine_ref.shape[0]
        dmine_ref[...] = dkv_ref[:keys_half]
        dtheirs_ref[...] = dkv_ref[keys_half:].astype(BF16)


def attend_back(pieces, out_weight, queries, mine, theirs, marks, stats, causal):
    length, width = queries.shape
    model = pieces[0].shape[1]
    keys_len = 2 * length
    heads = width // HEAD_DIM
    step = min(256, length)
    rows = pl.BlockSpec((step, width), lambda i: (i, 0))
    operands, specs = weight_specs([out_weight])
    return call(
        partial(attend_back_kernel, causal=causal, heads=heads), "attend_back",
        [((length, width), BF16), ((length, 2 * width), F32), ((length, 2 * width), BF16)],
        operands + far([queries, mine, theirs, *marks, stats]) + [*pieces], grid=(length // step,),
        in_specs=specs
        + [rows, whole(mine), whole(theirs)]
        + mask_specs(step, keys_len, marks[3].shape[0])
        + [pl.BlockSpec((heads, step), lambda i: (0, i))]
        + [whole(piece) for piece in pieces],
        out_specs=[rows, whole(mine), whole(mine)],
        scratch=[
            pltpu.VMEM((keys_len, 2 * width), BF16),
            pltpu.VMEM((keys_len, 2 * width), F32),
            pltpu.VMEM((step, width), BF16),
            pltpu.VMEM((length, model), BF16),
        ],
        flops=10 * length * keys_len * width, exps=length * keys_len * heads,
    )


def attend_grads_kernel(*refs, pieces):
    sources, (dq_ref, dkv_ref, o_ref, out_ref), scratch = refs[:-7], refs[-7:-3], refs[-3:]
    for i, count in enumerate(pieces):
        load(sources[:count], scratch[i])
        sources = sources[count:]
    xq_ref, g_ref = scratch[0], scratch[1]
    xkv_ref = scratch[2] if len(pieces) > 2 else xq_ref
    shard = out_ref.shape[2]
    for index, (cols_ref, at, rhs_ref) in enumerate(
        ((dq_ref, 0, xq_ref), (dkv_ref, 0, xkv_ref), (dkv_ref, 2 * shard, xkv_ref), (o_ref, 0, g_ref))
    ):
        both = dot(cols_ref[:, at : at + 2 * shard], rhs_ref[...], TN).astype(BF16)
        out_ref[0, index] = both[:shard]
        out_ref[1, index] = both[shard:]


def attend_grads(grad_q, grad_kv, mixed, *sources):
    length, model = rows_of(sources[0])
    shard = mixed.shape[1] // 2
    return call(
        partial(attend_grads_kernel, pieces=[len(source) for source in sources]), "attend_grads",
        [((2, 4, shard, model), BF16)], [piece for source in sources for piece in source] + [grad_q, grad_kv, far(mixed)],
        scratch=[pltpu.VMEM((length, model), BF16)] * 3, flops=16 * length * model * shard,
    )[0]


def gelu_pair(pre_act):
    phi_big = 0.5 * (1.0 + lax.erf(pre_act * (1.0 / math.sqrt(2.0))))
    phi_small = jnp.exp(-0.5 * pre_act * pre_act) * (1.0 / math.sqrt(2.0 * math.pi))
    return pre_act * phi_big, phi_big + pre_act * phi_small


def ffn_step(total, acc_ref, out_refs):
    step = pl.program_id(0)

    @pl.when(step == 0)
    def _():
        acc_ref[...] = total

    @pl.when(step > 0)
    def _():
        acc_ref[...] += total

    @pl.when(step == pl.num_programs(0) - 1)
    def _():
        fill(out_refs, acc_ref)


def ffn_kernel(up_ref, up2_ref, dn_ref, dn2_ref, *refs, pieces):
    sources, (act_ref, slope_ref), out_refs, (acc_ref, x_ref) = refs[:pieces], refs[pieces : pieces + 2], refs[pieces + 2 : -2], refs[-2:]

    @pl.when(pl.program_id(0) == 0)
    def _():
        load(sources, x_ref)

    total = None
    for side, (up, down) in enumerate(((up_ref, dn_ref), (up2_ref, dn2_ref))):
        act, slope = gelu_pair(dot(x_ref[...], up[...], NN))
        act = act.astype(BF16)
        act_ref[side] = act
        slope_ref[side] = slope
        term = dot(act, flat(down), NN)
        total = term if total is None else total + term
    ffn_step(total, acc_ref, out_refs)


def ffn_specs(pieces, ups, downs):
    length, model = rows_of(pieces)
    hidden = ups[0].shape[1]
    step = min(256, hidden)
    cols = pl.BlockSpec((model, step), lambda i: (0, i))
    rows = pl.BlockSpec((step, model), lambda i: (i, 0))
    other_rows = rows
    if downs[1].ndim == 3:
        share = hidden // downs[1].shape[0]
        other_rows = pl.BlockSpec((step // share, share, model), lambda i: (i, 0, 0))
    made = pl.BlockSpec((2, length, step), lambda i: (0, 0, i))
    scratch = [pltpu.VMEM((length, model), F32), pltpu.VMEM((length, model), BF16)]
    return length, model, hidden, step, [cols, cols, rows, other_rows], made, [whole(piece) for piece in pieces], scratch


def ffn(pieces, ups, downs, group):
    length, model, hidden, step, specs, made, piece_specs, scratch = ffn_specs(pieces, ups, downs)
    outs, out_specs = block_outs(length, model, group)
    acts, slopes, *parts = call(
        partial(ffn_kernel, pieces=len(pieces)), "ffn",
        [((2, length, hidden), BF16), ((2, length, hidden), F32)] + outs,
        [*far(ups), *far(downs), *pieces], grid=(hidden // step,), in_specs=specs + piece_specs,
        out_specs=[made, made] + out_specs, scratch=scratch, flops=8 * length * model * hidden, exps=4 * length * hidden,
    )
    return parts, acts, slopes


def ffn_back_kernel(up_ref, up2_ref, dn_ref, dn2_ref, slope_ref, *refs, pieces):
    sources, dz_ref, out_refs, (acc_ref, g_ref) = refs[:pieces], refs[pieces], refs[pieces + 1 : -2], refs[-2:]

    @pl.when(pl.program_id(0) == 0)
    def _():
        load(sources, g_ref)

    total = None
    for side, (up, down) in enumerate(((up_ref, dn_ref), (up2_ref, dn2_ref))):
        grad_pre = (slope_ref[side] * dot(g_ref[...], flat(down), NT)).astype(BF16)
        dz_ref[side] = grad_pre
        term = dot(grad_pre, up[...], NT)
        total = term if total is None else total + term
    ffn_step(total, acc_ref, out_refs)


def ffn_back(pieces, ups, downs, slopes, group):
    length, model, hidden, step, specs, made, piece_specs, scratch = ffn_specs(pieces, ups, downs)
    outs, out_specs = block_outs(length, model, group)
    grad_pre, *parts = call(
        partial(ffn_back_kernel, pieces=len(pieces)), "ffn_back", [((2, length, hidden), BF16)] + outs,
        [*far(ups), *far(downs), far(slopes), *pieces], grid=(hidden // step,), in_specs=specs + [made] + piece_specs,
        out_specs=[made] + out_specs, scratch=scratch, flops=8 * length * model * hidden,
    )
    return parts, grad_pre


def ffn_grads_kernel(dz_ref, act_ref, *refs):
    sources, (out_ref, x_ref, g_ref) = refs[:-3], refs[-3:]

    @pl.when((pl.program_id(0) == 0) & (pl.program_id(1) == 0))
    def _():
        load(sources[: len(sources) // 2], x_ref)
        load(sources[len(sources) // 2 :], g_ref)

    out_ref[0, 0] = dot(dz_ref[0], x_ref[...], TN).astype(BF16)
    out_ref[0, 1] = dot(act_ref[0], g_ref[...], TN).astype(BF16)


def ffn_grads(pieces, grads, grad_pre, acts):
    length, model = rows_of(pieces)
    hidden = acts.shape[2]
    step = min(256, hidden)
    made = pl.BlockSpec((1, length, step), lambda s, i: (s, 0, i))
    return call(
        ffn_grads_kernel, "ffn_grads", [((2, 2, hidden, model), BF16)], [grad_pre, far(acts), *far(pieces), *grads],
        grid=(2, hidden // step), in_specs=[made, made] + [whole(p) for p in (*pieces, *grads)],
        out_specs=[pl.BlockSpec((1, 2, step, model), lambda s, i: (s, 0, i, 0))],
        scratch=[pltpu.VMEM((length, model), BF16)] * 2, flops=8 * length * model * hidden,
    )[0]


class Places:
    def __init__(self):
        self.dp_size = lax.axis_size("dp")
        self.tensor_size = lax.axis_size("tensor")
        self.group = self.tensor_size // 2
        self.dp_index = lax.axis_index("dp")
        tensor_index = lax.axis_index("tensor")
        self.core = self.dp_index % 2
        self.place = tensor_index % self.group
        self.pieces = 2 if self.group == 4 else 1

    def swap(self, value):
        pairs = []
        for dp_index in range(self.dp_size):
            for tensor_index in range(self.tensor_size):
                pair, core = divmod(dp_index, 2)
                side, place = divmod(tensor_index, self.group)
                pairs.append(
                    (
                        dp_index * self.tensor_size + tensor_index,
                        (2 * pair + side) * self.tensor_size + core * self.group + place,
                    )
                )
        return lax.ppermute(value, ("dp", "tensor"), pairs)

    def other_core(self, value):
        return lax.ppermute(value, "dp", [(d, d ^ 1) for d in range(self.dp_size)])

    def partner(self, value):
        return lax.ppermute(value, "tensor", [(t, t ^ self.group) for t in range(self.tensor_size)])

    def mate(self, value, offset):
        return lax.ppermute(value, "tensor", [(t, t ^ offset) for t in range(self.tensor_size)])

    def gather(self, pieces):
        if self.pieces == 2:
            low, high = pieces
            low_1, high_2 = self.mate(low, 1), self.mate(high, 2)
            high_1, low_2 = self.mate(high, 1), self.mate(low, 2)
            high_3, low_3 = self.mate(high_2, 1), self.mate(low_1, 2)
            return [low, high, low_1, high_1, low_2, high_2, low_3, high_3]
        return list(pieces) + [self.mate(pieces[0], o) for o in range(1, self.group)]

    def gather_beside(self, block):
        return [block] + [self.mate(block, o) for o in range(1, self.group)]

    def scatter(self, parts):
        return [parts[0]] + [self.mate(parts[o], o) for o in range(1, self.group)]

    def share(self, stacked):
        rows = stacked.shape[0] // self.dp_size
        return lax.dynamic_slice_in_dim(stacked, self.dp_index * rows, rows, 0)

    def split(self, weights):
        rows = weights.shape[1] // self.dp_size
        return lax.dynamic_slice_in_dim(weights, self.dp_index * rows, rows, 1)

    def whole(self, share):
        return lax.all_gather(share, "dp", axis=0)

    def whole_rows(self, share):
        return lax.all_gather(share, "dp", axis=0, tiled=True)

    def sum_weights(self, grads):
        shape = grads.shape
        summed = lax.psum_scatter(grads.reshape(-1, shape[-1]), "dp", scatter_dimension=1, tiled=True)
        return summed.reshape(*shape[:-1], -1)

    def sum_weights_now(self, grads):
        if self.dp_size != 4:
            return self.sum_weights(grads)
        width = grads.shape[-1] // 4
        blocks = [grads[..., i * width : (i + 1) * width] for i in range(4)]
        first = self.core == 0

        def pick(if_first, low, high):
            return jnp.where(if_first, low, high)

        kept = jnp.concatenate([pick(first, *blocks[:2]), pick(first, *blocks[2:])], axis=-1)
        sent = jnp.concatenate([pick(first, *blocks[1::-1]), pick(first, *blocks[:1:-1])], axis=-1)
        kept = kept.astype(F32) + self.other_core(sent).astype(F32)
        low, high = kept[..., :width], kept[..., width:]
        first = self.dp_index < 2
        sent = pick(first, high, low).astype(BF16)
        received = lax.ppermute(sent, "dp", [(d, d ^ 2) for d in range(4)])
        return (pick(first, low, high) + received.astype(F32)).astype(BF16)

    def marks(self, seg_row, seg_key_row):
        kinds = jnp.arange(SEGMENTS)[:, None] - 1
        length = seg_row.shape[0] // self.tensor_size
        order = self.place ^ jnp.arange(self.group)
        blocks = jnp.concatenate([self.core * self.group + order, (1 - self.core) * self.group + order])
        own = jnp.take(seg_row.reshape(-1, length), blocks[: self.group], axis=0).reshape(1, -1)
        keys = jnp.take(seg_key_row.reshape(-1, length), blocks, axis=0).reshape(1, -1)
        positions = (blocks[: self.group, None] * length + jnp.arange(length)[None, :]).reshape(1, -1)
        return (
            ((own == kinds) | (own < 0)).astype(BF16),
            (keys == kinds).astype(BF16),
            positions,
            jnp.broadcast_to(blocks[:, None] * length, (blocks.shape[0], own.shape[1])),
        )


def route(places, token_ids, token_live, shard_rows):
    owners = places.dp_size * places.tensor_size
    tokens = token_ids.shape[0]
    capacity = max(2, 3 * tokens // (2 * owners))
    owner = token_ids // shard_rows
    row = token_ids - owner * shard_rows
    earlier = jnp.arange(tokens)[None, :] < jnp.arange(tokens)[:, None]
    same = (owner[:, None] == owner[None, :]) & token_live[None, :] & earlier
    ranking = jnp.sum(same.astype(jnp.int32), axis=1)
    slot = jnp.where(token_live, owner * capacity + ranking, -1)
    picks = jnp.arange(owners * capacity)[:, None] == slot[None, :]
    requests = jnp.sum(jnp.where(picks, row[None, :] + 1, 0), axis=1) - 1
    return picks.astype(BF16), requests.reshape(owners, capacity)


LANES = 128


def to_owners(places, rows, capacity):
    owners = places.dp_size * places.tensor_size
    runs = rows.reshape(owners, capacity * rows.shape[1] // LANES, LANES)
    return lax.all_to_all(runs, ("dp", "tensor"), split_axis=0, concat_axis=0, tiled=True)


def finish_kernel(*refs, count):
    parts, outs = refs[: 2 * count], refs[2 * count :]
    for i in range(count):
        own_ref, other_ref = parts[2 * i], parts[2 * i + 1]
        in_ref, out_ref = outs[2 * i], outs[2 * i + 1]
        for j in range(3):
            in_ref[j] = (own_ref[j].astype(F32) + other_ref[j].astype(F32)).T
        out_ref[...] = own_ref[3].astype(F32) + other_ref[3].astype(F32)


def finish_attention(*pairs):
    _, shard, width = pairs[0][0].shape
    return call(
        partial(finish_kernel, count=len(pairs)), "finish",
        [((3, width, shard), F32), ((shard, width), F32)] * len(pairs), [part for pair in pairs for part in pair],
    )


def finish_kernel(*refs, count):
    parts, outs = refs[: 2 * count], refs[2 * count :]
    for i in range(count):
        own_ref, other_ref = parts[2 * i], parts[2 * i + 1]
        in_ref, out_ref = outs[2 * i], outs[2 * i + 1]
        for j in range(3):
            in_ref[j] = (own_ref[j].astype(F32) + other_ref[j].astype(F32)).T
        out_ref[...] = own_ref[3].astype(F32) + other_ref[3].astype(F32)


def finish_attention(*pairs):
    _, shard, width = pairs[0][0].shape
    return call(
        partial(finish_kernel, count=len(pairs)), "finish",
        [((3, width, shard), F32), ((shard, width), F32)] * len(pairs), [part for pair in pairs for part in pair],
    )


def send_back_kernel(picks_ref, e_ref, e2_ref, last_ref, *refs):
    gain_refs, out_ref, rows_ref = refs[:-2], refs[-2], refs[-1]
    length = e_ref.shape[0]
    rows_ref[...] = jnp.zeros_like(rows_ref)
    for i, ref in enumerate(gain_refs):
        rows_ref[i : i + 1] = ref[...]
    sent = dot(picks_ref[:, :length], e_ref[...], NN) + dot(picks_ref[:, length:], e2_ref[...], NN)
    out_ref[...] = (sent + dot(last_ref[...], rows_ref[...].astype(BF16), NN)).astype(BF16)


def send_back(picks, src_grad, tgt_grad, gains, capacity):
    owners = picks.shape[0] // capacity
    slots = jnp.arange(owners * (capacity + 1))
    owner, slot = slots // (capacity + 1), slots % (capacity + 1)
    wider = jnp.take(picks, jnp.minimum(owner * capacity + slot, picks.shape[0] - 1), axis=0)
    wider = jnp.where((slot < capacity)[:, None], wider, jnp.zeros_like(wider))
    rows = 16
    last = (slot == capacity)[:, None] & (owner[:, None] == jnp.arange(rows)[None, :])
    return call(
        send_back_kernel, "send_back", [((slots.shape[0], src_grad.shape[1]), BF16)],
        [wider, src_grad, tgt_grad, last.astype(BF16), *gains], scratch=[pltpu.VMEM((rows, src_grad.shape[1]), F32)],
        flops=2 * wider.size * src_grad.shape[1],
    )[0]


def on_device(
    src_ids,
    tgt_ids,
    src_segs,
    tgt_segs,
    embed_table,
    norm_gains,
    enc_qkv,
    enc_out,
    enc_up,
    enc_down,
    dec_qkv,
    dec_out,
    cross_q,
    cross_kv,
    cross_out,
    dec_up,
    dec_down,
    cotangent,
):
    places = Places()
    group = places.group
    local_len = src_ids.shape[0]
    shard_rows, model = embed_table.shape
    root = math.sqrt(model)
    shard = enc_qkv.shape[2]
    count = places.pieces

    tensor_at = lax.axis_index("tensor") * local_len
    rows_here = [src_segs.reshape(-1), tgt_segs.reshape(-1)]
    ids_here = jnp.concatenate([src_ids.reshape(-1), tgt_ids.reshape(-1)])
    live_here = jnp.concatenate([lax.dynamic_slice_in_dim(row, tensor_at, local_len, 0) for row in rows_here]) >= 0
    enc_in_share = places.partner(places.split(enc_qkv))
    requests = route(places, ids_here, live_here, shard_rows)[1]
    capacity = requests.shape[1]
    moved = places.swap(jnp.concatenate([ids_here] + rows_here))
    wanted = lax.all_to_all(requests, ("dp", "tensor"), split_axis=0, concat_axis=0, tiled=True)
    wanted = wanted.reshape(-1, 2, 2, group * capacity).swapaxes(1, 2).reshape(-1)
    wanted = after(wanted, moved, enc_in_share)
    found = wanted >= 0
    picked = jnp.take(embed_table, jnp.maximum(wanted, 0), axis=0, mode="clip")
    replies = to_owners(places, picked, capacity).reshape(picked.shape)
    outs_share = jnp.concatenate([places.share(weight) for weight in (enc_out, dec_out, cross_out)])
    outs_share = places.partner(after(outs_share, picked))
    replies = after(replies, outs_share)
    cross_share = jnp.concatenate([places.split(cross_q[None]), places.split(cross_kv)])

    token_ids = moved[: 2 * local_len]
    src_row, tgt_row = jnp.split(moved[2 * local_len :], 2)
    offset = (places.core * group + places.place) * local_len
    live = [lax.dynamic_slice_in_dim(row, offset, local_len, 0) >= 0 for row in (src_row, tgt_row)]
    picks = route(places, token_ids, jnp.concatenate(live), shard_rows)[0]
    enc_marks = places.marks(src_row, src_row)
    dec_marks = places.marks(tgt_row, tgt_row)
    cross_marks = places.marks(tgt_row, src_row)

    def narrow(own, own_index, other, other_index):
        if own.ndim == 2:
            own_part = (own, own.shape, (0, 0))
        else:
            own_part = (own, (1, *own.shape[1:]), (own_index, 0, 0))
        return own_part, (other, (other.shape[0], 1, *other.shape[2:]), (0, other_index, 0, 0))

    def wide(own, other, index):
        rows = own.shape[0] // places.dp_size
        return (own, own.shape, (0, 0)), (other, (other.shape[0], rows, model), (0, index, 0))

    def narrow_whole(share, start):
        share = after(share, start)
        return places.whole(jnp.concatenate([share, share]))

    enc_in_other = narrow_whole(enc_in_share, picked)
    enc_in = [narrow(enc_qkv, i, enc_in_other, i) for i in range(3)]

    token_shape = (local_len, model)
    embeds, h0, t0, *pieces = call(
        partial(embed_kernel, root=root), "embed",
        [((2 * local_len, model), BF16), (token_shape, F32), (token_shape, F32)] + [((local_len // count, model), BF16)] * count + [(token_shape, BF16)],
        [picks, replies, norm_gains],
    )
    a1, c1 = pieces[:-1], pieces[-1]
    down_rows = enc_down.shape[0] // places.dp_size
    out_rows = shard // places.dp_size
    outs_other = narrow_whole(outs_share, a1)
    dec_in_share = places.partner(after(places.split(dec_qkv), a1))
    a1 = places.gather(a1)
    c1 = places.gather_beside(after(c1, a1))
    out_rows = shard // places.dp_size
    if out_rows % 8:
        outs_other = [outs_other[:, i * out_rows : (i + 1) * out_rows] for i in range(3)]
        enc_o, dec_o, cross_o = [wide(own, other, 0) for own, other in zip((enc_out, dec_out, cross_out), outs_other)]
    else:
        enc_o, dec_o, cross_o = [wide(own, outs_other, i) for i, own in enumerate((enc_out, dec_out, cross_out))]
    enc_q, enc_mine = project(a1, enc_in, shard, True)
    dec_in_other = narrow_whole(dec_in_share, enc_mine)
    dec_in = [narrow(dec_qkv, i, dec_in_other, i) for i in range(3)]
    enc_theirs = places.other_core(enc_mine)
    parts, enc_mixed, enc_stats = attend(enc_q, enc_mine, enc_theirs, enc_o, enc_marks, False, model, group)
    enc_up_share = places.partner(after(places.share(enc_up), enc_mine))
    enc_down_share = places.partner(after(places.share(enc_down), enc_mine))
    own_parts = after(parts, enc_up_share, c1)
    enc_ups = [enc_up, places.whole_rows(after(enc_up_share, own_parts))]
    parts = places.scatter(own_parts)
    dec_q, dec_mine = project(after(c1, own_parts), dec_in, shard, True)
    dec_theirs = places.other_core(dec_mine)
    cross_share = places.partner(after(cross_share, dec_mine))
    cot_moved = places.swap(after(cotangent.reshape(token_shape).astype(BF16), dec_mine))
    dec_parts, dec_mixed, dec_stats = attend(
        after(dec_q, enc_down_share), dec_mine, dec_theirs, dec_o, dec_marks, True, model, group
    )
    enc_downs = [enc_down, places.whole_rows(after(enc_down_share, dec_q))]
    h1, own_b1 = sum_norm(h0, after(parts, dec_parts, cot_moved), norm_gains, 2, count)

    b1 = places.gather(own_b1)
    cross_other = narrow_whole(cross_share, own_b1)
    dec_parts = places.scatter(after(dec_parts, own_b1))
    t1, (own_c2,) = sum_norm(t0, after(dec_parts, b1), norm_gains, 6, 1)
    dec_up_share = places.partner(after(places.share(dec_up), own_c2))
    b1 = after(b1, own_c2)
    c2 = places.gather_beside(own_c2)
    own_parts, enc_acts, enc_slopes = ffn(b1, enc_ups, enc_downs, group)
    own_parts = after(own_parts, c2)
    cross_in = narrow(cross_q, 0, cross_other, 0)
    cross_mem = [narrow(cross_kv, i, cross_other, 1 + i) for i in range(2)]
    parts = places.scatter(own_parts)
    h2, own_memory = sum_norm(h1, parts, norm_gains, 3, count)
    dec_ups = [dec_up, places.whole_rows(after(dec_up_share, own_memory))]
    memory = places.gather(own_memory)
    cross_qs = project(after(c2, own_memory), [cross_in], shard, True)[0]
    cross_mine = project(after(memory, cross_qs), cross_mem, shard, False)[0]
    dec_down_share = places.partner(after(places.share(dec_down), cross_mine))
    cross_theirs = places.other_core(cross_mine)
    parts, cross_mixed, cross_stats = attend(
        cross_qs, cross_mine, cross_theirs, cross_o, cross_marks, False, model, group
    )
    dec_downs = [dec_down, places.whole_rows(after(dec_down_share, parts))]
    t2, own_f1 = sum_norm(t1, places.scatter(parts), norm_gains, 7, count)
    f1 = places.gather(own_f1)
    parts, dec_acts, dec_slopes = ffn(f1, dec_ups, dec_downs, group)
    decoded, grad_t, pieces, gain_final = final(
        t2, places.scatter(parts), norm_gains, live[1][:, None].astype(F32), cot_moved, 8, count
    )

    grad_full = places.gather(pieces)
    decoded = places.swap(after(decoded, grad_full))
    own_parts, grad_pre = ffn_back(grad_full, dec_ups, dec_downs, dec_slopes, group)
    dec_ffn_grads = ffn_grads(f1, after(grad_full, own_parts), grad_pre, dec_acts)
    parts = after(places.scatter(own_parts), dec_ffn_grads)
    grad_t, pieces, gain_dffn = norm_back(grad_t, parts, t2, norm_gains, 7, count)

    dec_ffn_sum = places.sum_weights(after(dec_ffn_grads, pieces))
    grad_full = after(places.gather(pieces), decoded)
    grad_q, mine, theirs = attend_back(
        grad_full, cross_o, cross_qs, cross_mine, cross_theirs, cross_marks, cross_stats, False
    )
    theirs = places.other_core(theirs)
    own_parts = unproject(grad_q, cross_in, model, group)
    own_mem_parts, grad_kv = unproject_keys(None, mine, after(theirs, own_parts), cross_mem, model, group)
    mem_parts = places.scatter(own_mem_parts)
    cross_grads = attend_grads(grad_q, grad_kv, cross_mixed, far(c2), after(grad_full, own_mem_parts), far(memory))
    grad_h, pieces_h, gain_memory = norm_back(None, after(mem_parts, cross_grads), h2, norm_gains, 3, count)
    cross_sum = places.sum_weights(after(cross_grads, pieces_h))

    def finish(summed, other):
        return summed[0].astype(F32) + other.astype(F32)

    def turned(grads):
        return jnp.swapaxes(grads, -1, -2)

    enc_full = places.gather(pieces_h)
    parts = places.scatter(after(own_parts, enc_full))
    dec_ffn_other = places.partner(after(dec_ffn_sum[1], enc_full))
    own_parts, grad_pre = ffn_back(enc_full, enc_ups, enc_downs, enc_slopes, group)
    h_parts = places.scatter(own_parts)
    enc_ffn_grads = ffn_grads(b1, after(enc_full, own_parts), grad_pre, enc_acts)
    grad_t, pieces, gain_cross = norm_back(grad_t, after(parts, enc_ffn_grads, dec_ffn_sum), t1, norm_gains, 6, count)
    dec_full = places.gather(pieces)
    grad_h, pieces_h, gain_effn = norm_back(grad_h, after(h_parts, pieces), h1, norm_gains, 2, 1)
    hidden_full = places.gather_beside(pieces_h[0])
    dec_full = after(dec_full, pieces_h, dec_ffn_other)
    cross_sum_other = places.partner(after(cross_sum[1], dec_full))
    enc_ffn_sum = places.sum_weights(after(enc_ffn_grads, cross_sum, pieces_h))
    grad_q, mine, theirs = attend_back(dec_full, dec_o, dec_q, dec_mine, dec_theirs, dec_marks, dec_stats, True)
    theirs = places.other_core(theirs)
    own_parts, grad_kv = unproject_keys(grad_q, mine, theirs, dec_in, model, group)
    dec_parts = places.scatter(own_parts)
    dec_grads = attend_grads(grad_q, grad_kv, dec_mixed, far(c1), after(dec_full, own_parts))

    grad_full = after(hidden_full, dec_grads, cross_sum_other)
    grad_q, mine, theirs = attend_back(grad_full, enc_o, enc_q, enc_mine, enc_theirs, enc_marks, enc_stats, False)
    theirs = places.other_core(theirs)
    dec_sum = places.sum_weights(after(dec_grads, enc_ffn_sum, grad_full))
    own_parts, grad_kv = unproject_keys(grad_q, mine, theirs, enc_in, model, group)
    parts = places.scatter(own_parts)
    dec_ffn_sum = finish(dec_ffn_sum, dec_ffn_other)
    dec_ffn_outs = turned(dec_ffn_sum[0]), dec_ffn_sum[1]
    cross_sum = finish(cross_sum, cross_sum_other)
    cross_outs = turned(cross_sum[0]), turned(cross_sum[1:3]), cross_sum[3]
    decoded_out = decoded.astype(F32)[:, None]
    dec_ffn_outs, cross_outs, decoded_out = lax.optimization_barrier((dec_ffn_outs, cross_outs, decoded_out))
    tgt_grad, gain_dattn, gain_demb = embed_back(
        grad_t, after(dec_parts, own_parts, dec_ffn_outs, cross_outs, decoded_out), t0, embeds[local_len:], norm_gains, 4, root
    )
    src_grad, gain_eattn, gain_eemb = embed_back(
        grad_h, after(parts, tgt_grad), h0, embeds[:local_len], norm_gains, 0, root
    )

    gains = [
        gain_eemb, gain_eattn, gain_effn, gain_memory, gain_demb, gain_dattn, gain_cross, gain_dffn, gain_final
    ]
    outgoing = send_back(picks, src_grad, tgt_grad, gains, capacity)
    arrived = to_owners(places, outgoing, capacity + 1)
    enc_grads = attend_grads(grad_q, grad_kv, enc_mixed, far(a1), after(grad_full, outgoing))
    enc_sum = places.sum_weights_now(enc_grads)
    enc_ffn_other = places.partner(after(enc_ffn_sum[1], outgoing))
    arrived = after(arrived, enc_sum, enc_ffn_other)
    last_other = places.partner(after(jnp.stack([dec_sum[1], enc_sum[1]]), arrived))
    slots = capacity * model // LANES
    gain_sum = jnp.sum(arrived[:, slots:].astype(F32), axis=0).reshape(model)
    gain_grad = lax.all_to_all(
        jnp.broadcast_to(gain_sum[None], (arrived.shape[0], model)), ("dp", "tensor"), 0, 0, tiled=True
    )[: len(gains)]
    counts = jnp.sum(((wanted[:, None] == wanted[None, :]) & found[None, :]).astype(F32), axis=1)
    rows = arrived[:, :slots].reshape(-1, model).astype(F32) / jnp.maximum(counts, 1.0)[:, None]
    target_rows = jnp.where(found, wanted, shard_rows)
    table_grad = jnp.zeros((shard_rows, model), F32).at[target_rows].add(rows, mode="drop")

    enc_ffn_sum = finish(enc_ffn_sum, enc_ffn_other)
    dec_in_grad, dec_out_grad, enc_in_grad, enc_out_grad = finish_attention(
        (dec_sum[0], last_other[0]), (enc_sum[0], last_other[1])
    )

    return (
        decoded_out,
        table_grad,
        gain_grad,
        enc_in_grad,
        enc_out_grad,
        turned(enc_ffn_sum[0]),
        enc_ffn_sum[1],
        dec_in_grad,
        dec_out_grad,
        *cross_outs,
        *dec_ffn_outs,
    )


def solution(mesh):
    return jax.shard_map(
        on_device,
        mesh=mesh,
        in_specs=(
            P("tensor", "dp"),
            P("tensor", "dp"),
            P(None, "dp"),
            P(None, "dp"),
            P(("dp", "tensor"), None),
            P(),
            P(None, None, "tensor"),
            P("tensor", None),
            P(None, "tensor"),
            P("tensor", None),
            P(None, None, "tensor"),
            P("tensor", None),
            P(None, "tensor"),
            P(None, None, "tensor"),
            P("tensor", None),
            P(None, "tensor"),
            P("tensor", None),
            P("tensor", "dp", None),
        ),
        out_specs=(
            P("tensor", "dp", None),
            P(("dp", "tensor"), None),
            P(),
            P(None, "dp", "tensor"),
            P("tensor", "dp"),
            P("dp", "tensor"),
            P("tensor", "dp"),
            P(None, "dp", "tensor"),
            P("tensor", "dp"),
            P("dp", "tensor"),
            P(None, "dp", "tensor"),
            P("tensor", "dp"),
            P("dp", "tensor"),
            P("tensor", "dp"),
        ),
        check_vma=False,
    )
```
